512 devices in a mesh: frame: 8 (over x, core), row: 32 (over z_lo, y), head: 2 (over z_hi).
Axes of the slice: x: 4, y: 8, z: 8 (z_hi: 2, z_lo: 4; z = z_hi * 4 + z_lo), core: 2. Of those that a mesh axis runs over, the one named last changes fastest.
Arguments:
- q_pre: bfloat16 [8, 64, 64, 2560], P('frame', 'row', None, 'head'), may hold values from -60 to 60
- k_pre: bfloat16 [8, 64, 64, 2560], P('frame', 'row', None, 'head'), may hold values from -60 to 60
- values: bfloat16 [8, 64, 64, 2560], P('frame', 'row', None, 'head'), may hold values from -6 to 6
- target: bfloat16 [8, 64, 64, 2560], P('frame', 'row', None, 'head'), may hold values from -6 to 6
- gain_q: float32 [2560], P('head'), may hold values from 0.5 to 2
- gain_k: float32 [2560], P('head'), may hold values from 0.5 to 2
- kept: int32 [8, 64, 4], replicated, may hold values 0 or 1
Outputs:
- grad_q: bfloat16 [8, 64, 64, 2560], P('frame', 'row', None, 'head')
- grad_k: bfloat16 [8, 64, 64, 2560], P('frame', 'row', None, 'head')
- grad_v: bfloat16 [8, 64, 64, 2560], P('frame', 'row', None, 'head')
The draws below stay inside these ranges and needn't reach their ends.
All inputs are finite; a program needn't handle non-finite values.
Results may differ from the reference program's by a relative error of at most 0.0107.
The reference program's roundings to bfloat16 on the way (of `prob_b`, `d_out` and `score_grad`) count: a program that leaves them out, or rounds other values in their place, can miss the bound.
Values may be sent and summed in bfloat16 or wider, within the bound.
A program may use at most 128 MiB of HBM per device.

```python
import math
import jax
import jax.numpy as jnp
from jax import lax

CW = 64
TC = 16
HEADS = 20
HD = 128
NF = 8
NR = 64
NCT = 4
FEAT = 2560


def scaled_pair(key):
    count = NF * NR * CW
    features = HEADS * HD
    head_of = jnp.arange(features) // HD
    jitter = jax.random.uniform(jax.random.fold_in(key, 11), (HEADS,))
    head_scale = 0.3 * 10.0 ** ((jnp.arange(HEADS) + jitter) / HEADS)
    column_scale = jnp.sum((head_of[:, None] == jnp.arange(HEADS)[None, :]) * head_scale[None, :], axis=1)
    rows_k = jnp.exp(jax.random.uniform(jax.random.fold_in(key, 12), (count, 1), minval=jnp.log(0.5), maxval=jnp.log(5.0)))
    rows_q = jnp.exp(jax.random.uniform(jax.random.fold_in(key, 13), (count, 1), minval=jnp.log(0.5), maxval=jnp.log(5.0)))
    base_k = jax.random.truncated_normal(jax.random.fold_in(key, 14), -4.0, 4.0, (count, features))
    base_q = jax.random.truncated_normal(jax.random.fold_in(key, 15), -4.0, 4.0, (count, features))
    keys_all = base_k * column_scale[None, :] * rows_k
    queries_all = base_q * column_scale[None, :] * rows_q
    shape = (NF, NR, CW, features)
    return (queries_all.reshape(shape), keys_all.reshape(shape))


def draw_q_pre(key, part):
    return scaled_pair(key)[0].astype(jnp.bfloat16)


def draw_k_pre(key, part):
    return scaled_pair(key)[1].astype(jnp.bfloat16)


def touch_ends(values, key, low, top_value):
    longest = values.shape.index(max(values.shape))
    spots = []
    for shift in (0, 1):
        where = [jax.random.randint(jax.random.fold_in(key, axis), (), 0, length) for axis, length in enumerate(values.shape)]
        where[longest] = (where[longest] + shift) % values.shape[longest]
        spots.append(tuple(where))
    return values.at[spots[0]].set(low).at[spots[1]].set(top_value)


def block_scale(rng, dims, split, least, top_value):
    loudness, own = 1.0, jax.random.fold_in(rng, 6)
    for position, blocks in split:
        heights = jnp.exp(jax.random.uniform(jax.random.fold_in(own, position), (blocks,), jnp.float32, least / len(split), top_value / len(split)))
        loudness = loudness * jnp.repeat(heights, dims[position] // blocks).reshape([-1 if axis == position else 1 for axis in range(len(dims))])
    return loudness


def bell_draw(key, shape, width, bound, pieces=(), kind=jnp.bfloat16):
    result = width * jax.random.normal(key, shape, jnp.float32)
    if pieces:
        result = result * block_scale(key, shape, pieces, -0.22, 0.18)
    return jnp.clip(result, -bound, bound).astype(kind)


def setup_inputs(seed: int = 0) -> dict:
    streams_of = jax.random.split(jax.random.key(seed), 8)
    q_pre = draw_q_pre(jax.random.fold_in(streams_of[7], 71), 0)
    k_pre = draw_k_pre(jax.random.fold_in(streams_of[7], 71), 0)
    values = bell_draw(streams_of[2], (NF, NR, CW, FEAT), 1.0, 6.0, ((0, 8), (1, 32), (3, 2)))
    target = bell_draw(streams_of[3], (NF, NR, CW, FEAT), 1.0, 6.0, ((0, 8), (1, 32), (3, 2)))
    gain_q = jnp.clip(jnp.exp(math.log(2.0) - 1.3862944 * jax.random.uniform(streams_of[4], (FEAT,), jnp.float32) ** block_scale(streams_of[4], (FEAT,), ((0, 2),), -0.2, 0.2)), 0.5, 2.0)
    gain_k = jnp.clip(jnp.exp(math.log(2.0) - 1.3862944 * jax.random.uniform(streams_of[5], (FEAT,), jnp.float32) ** block_scale(streams_of[5], (FEAT,), ((0, 2),), -0.2, 0.2)), 0.5, 2.0)
    kept = touch_ends((jax.random.randint(streams_of[6], (NF, NR, NCT), 0, 4) < 3).astype(jnp.int32), jax.random.fold_in(streams_of[6], 1), 0, 1)
    return dict(q_pre=q_pre, k_pre=k_pre, values=values, target=target, gain_q=gain_q, gain_k=gain_k, kept=kept)


norm_eps = 1e-06

def window_mask(kept_win, col_tile, tiles):
    near_cols = jnp.abs(col_tile[:, None] - col_tile[None, :]) <= 1
    same_tile = col_tile[:, None] == col_tile[None, :]
    one_hot = col_tile[:, None] == jnp.arange(tiles)[None, :]
    key_kept = jnp.any(one_hot[None, None] & (kept_win[:, :, None, :] > 0), axis=-1)
    centre = (jnp.arange(3)[:, None] == 1) & (jnp.arange(3)[None, :] == 1)
    allowed = near_cols[:, None, None, :] & (key_kept[None] | centre[None, :, :, None] & same_tile[:, None, None, :])
    return allowed.reshape(col_tile.shape[0], -1)

def key_mask(kept_own, valid_win, col_tile, tiles):
    near_cols = jnp.abs(col_tile[:, None] - col_tile[None, :]) <= 1
    same_tile = col_tile[:, None] == col_tile[None, :]
    one_hot = col_tile[:, None] == jnp.arange(tiles)[None, :]
    own_kept = jnp.any(one_hot & (kept_own[None, :] > 0), axis=-1)
    centre = (jnp.arange(3)[:, None] == 1) & (jnp.arange(3)[None, :] == 1)
    allowed = near_cols[None, None] & (own_kept[None, None, None, :] | centre[:, :, None, None] & same_tile[None, None]) & valid_win[:, :, None, None]
    return allowed.reshape(-1, col_tile.shape[0])

def reference(q_pre, k_pre, values, target, gain_q, gain_k, kept):
    features = HEADS * HD
    score_scale = HD ** (-0.5)
    q_float = q_pre.astype(jnp.float32)
    k_float = k_pre.astype(jnp.float32)
    scale_q = lax.rsqrt(lax.optimization_barrier(jnp.sum(q_float * q_float, -1, keepdims=True)) / features + norm_eps)
    scale_k = lax.rsqrt(lax.optimization_barrier(jnp.sum(k_float * k_float, -1, keepdims=True)) / features + norm_eps)
    q_norm = (q_float * scale_q * gain_q).astype(jnp.bfloat16)
    k_norm = (k_float * scale_k * gain_k).astype(jnp.bfloat16)
    col_tile = jnp.arange(CW) // TC
    pad_two = ((1, 1), (1, 1), (0, 0), (0, 0))
    kv_pad = jnp.stack([jnp.pad(k_norm, pad_two), jnp.pad(values, pad_two)])
    kept_pad = jnp.pad(kept, ((1, 1), (1, 1), (0, 0)))
    line_ids = jnp.arange(NF * NR, dtype=jnp.int32)
    q_lines = q_norm.reshape(NF * NR, CW, features)
    t_lines = target.reshape(NF * NR, CW, features)

    def query_pass(line):
        f_at = (line // NR).astype(jnp.int32)
        r_at = (line % NR).astype(jnp.int32)
        zero = jnp.int32(0)
        query = lax.dynamic_index_in_dim(q_lines, line, 0, False).reshape(CW, HEADS, HD).astype(jnp.float32)
        t_line = lax.dynamic_index_in_dim(t_lines, line, 0, False).reshape(CW, HEADS, HD).astype(jnp.float32)
        kv_win = lax.dynamic_slice(kv_pad, (zero, f_at, r_at, zero, zero), (2, 3, 3, CW, features))
        kept_win = lax.dynamic_slice(kept_pad, (f_at, r_at, zero), (3, 3, NCT))
        allowed = window_mask(kept_win, col_tile, NCT)
        key_block = kv_win[0].reshape(9 * CW, HEADS, HD).astype(jnp.float32)
        value_block = kv_win[1].reshape(9 * CW, HEADS, HD).astype(jnp.float32)
        scores = jnp.einsum('qhd,khd->hqk', query, key_block) * score_scale
        scores = jnp.where(allowed[None], scores, -jnp.inf)
        row_max = lax.optimization_barrier(jnp.max(scores, -1, keepdims=True))
        expo = jnp.where(allowed[None], jnp.exp(scores - row_max), 0.0)
        denominator = lax.optimization_barrier(jnp.sum(expo, -1, keepdims=True))
        probability = expo / denominator
        prob_b = probability.astype(jnp.bfloat16)
        attended = jnp.einsum('hqk,khd->qhd', prob_b.astype(jnp.float32), value_block)
        d_out = (attended - t_line).astype(jnp.bfloat16)
        delta_sum = lax.optimization_barrier(jnp.sum(d_out.astype(jnp.float32) * attended, -1)).T
        prob_grad = jnp.einsum('qhd,khd->hqk', d_out.astype(jnp.float32), value_block)
        score_grad = (probability * (prob_grad - delta_sum[:, :, None]) * score_scale).astype(jnp.bfloat16)
        dq_line = jnp.einsum('hqk,khd->qhd', score_grad.astype(jnp.float32), key_block)
        log_total = row_max[..., 0] + jnp.log(denominator[..., 0])
        return (dq_line.reshape(CW, features), d_out.reshape(CW, features), log_total, delta_sum)
    dq_lines, dout_lines, total_lines, delta_lines = lax.map(query_pass, line_ids)
    d_out_grid = dout_lines.reshape(NF, NR, CW, features)
    stat_grid = jnp.stack([total_lines.reshape(NF, NR, HEADS, CW), delta_lines.reshape(NF, NR, HEADS, CW)])
    qd_pad = jnp.stack([jnp.pad(q_norm, pad_two), jnp.pad(d_out_grid, pad_two)])
    stat_pad = jnp.pad(stat_grid, ((0, 0), (1, 1), (1, 1), (0, 0), (0, 0)))
    valid_pad = jnp.pad(jnp.ones((NF, NR), dtype=bool), ((1, 1), (1, 1)))
    k_lines = k_norm.reshape(NF * NR, CW, features)
    v_lines = values.reshape(NF * NR, CW, features)

    def key_pass(line):
        f_at = (line // NR).astype(jnp.int32)
        r_at = (line % NR).astype(jnp.int32)
        zero = jnp.int32(0)
        key_own = lax.dynamic_index_in_dim(k_lines, line, 0, False).reshape(CW, HEADS, HD).astype(jnp.float32)
        value_own = lax.dynamic_index_in_dim(v_lines, line, 0, False).reshape(CW, HEADS, HD).astype(jnp.float32)
        qd_win = lax.dynamic_slice(qd_pad, (zero, f_at, r_at, zero, zero), (2, 3, 3, CW, features))
        stat_win = lax.dynamic_slice(stat_pad, (zero, f_at, r_at, zero, zero), (2, 3, 3, HEADS, CW))
        valid_win = lax.dynamic_slice(valid_pad, (f_at, r_at), (3, 3))
        kept_own = lax.dynamic_slice(kept, (f_at, r_at, zero), (1, 1, NCT)).reshape(NCT)
        allowed = key_mask(kept_own, valid_win, col_tile, NCT)
        query_win = qd_win[0].reshape(9 * CW, HEADS, HD).astype(jnp.float32)
        dout_win = qd_win[1].reshape(9 * CW, HEADS, HD).astype(jnp.float32)
        total_win = jnp.transpose(stat_win[0], (2, 0, 1, 3)).reshape(HEADS, 9 * CW)
        delta_win = jnp.transpose(stat_win[1], (2, 0, 1, 3)).reshape(HEADS, 9 * CW)
        scores = jnp.einsum('qhd,khd->hqk', query_win, key_own) * score_scale
        probability = jnp.where(allowed[None], jnp.exp(scores - total_win[:, :, None]), 0.0)
        prob_b = probability.astype(jnp.bfloat16)
        prob_grad = jnp.einsum('qhd,khd->hqk', dout_win, value_own)
        score_grad = (probability * (prob_grad - delta_win[:, :, None]) * score_scale).astype(jnp.bfloat16)
        dk_line = jnp.einsum('hqk,qhd->khd', score_grad.astype(jnp.float32), query_win)
        dv_line = jnp.einsum('hqk,qhd->khd', prob_b.astype(jnp.float32), dout_win)
        return (dk_line.reshape(CW, features), dv_line.reshape(CW, features))
    dk_lines, dv_lines = lax.map(key_pass, line_ids)
    dq_norm = dq_lines.reshape(NF, NR, CW, features)
    dk_norm = dk_lines.reshape(NF, NR, CW, features)
    grad_v = dv_lines.reshape(NF, NR, CW, features).astype(jnp.bfloat16)
    gated_q = gain_q * dq_norm
    gated_k = gain_k * dk_norm
    sum_q = lax.optimization_barrier(jnp.sum(q_float * gated_q, -1, keepdims=True))
    sum_k = lax.optimization_barrier(jnp.sum(k_float * gated_k, -1, keepdims=True))
    grad_q = (scale_q * gated_q - q_float * scale_q ** 3 * sum_q / features).astype(jnp.bfloat16)
    grad_k = (scale_k * gated_k - k_float * scale_k ** 3 * sum_k / features).astype(jnp.bfloat16)
    return (grad_q, grad_k, grad_v)
```

```python
import functools

import jax
import jax.numpy as jnp
from jax import lax
from jax.experimental import pallas as pl
from jax.experimental.pallas import tpu as pltpu
from jax.sharding import PartitionSpec as P

TC = 16
HD = 128
TILES = 4
MESH = pl.DeviceIdType.MESH
norm_eps = 1e-06
LOG2E = 1.4426950408889634
SCORE_SCALE = HD ** (-0.5)
NEG = -1e30

BF16 = jnp.bfloat16
F32 = jnp.float32
ROWS_T = (((0,), (0,)), ((), ()))
COLS_T = (((1,), (1,)), ((), ()))
PLAIN = (((1,), (0,)), ((), ()))


def dot(a, b, dims):
    return lax.dot_general(a, b, dims, preferred_element_type=F32)


def columns_to_rows(col_a, col_b):
    lane = lax.broadcasted_iota(jnp.int32, (128, 128), 1)
    both = jnp.where(lane < 4, jnp.broadcast_to(col_a, (128, 128)), jnp.broadcast_to(col_b, (128, 128)))
    return both.T[0:8]


def rows_to_columns(rows):
    sub = lax.broadcasted_iota(jnp.int32, (128, 128), 0)
    both = jnp.where(
        sub < 64,
        jnp.broadcast_to(rows[0:1], (128, 128)),
        jnp.broadcast_to(rows[4:5], (128, 128)),
    ).T
    return both[:, 0:1], both[:, 64:65]


def kernel(
    sizes, features, q_ref, k_ref, v_ref, t_ref, gq_ref, gk_ref, kept_ref,
    oq_ref, ok_ref, ov_ref,
    kv, qn, bias, gx_out, gx_in, gy_out, gy_in, own, dq, acc, hx_out, hx_in,
    row_s, row_r, fr_s, fr_r, co_s, co_r, gx_s, gx_r, gy_s, gy_r, hx_s, hx_r,
):
    frames, rows, heads = sizes
    chunks, _, _, _, width, wide = kv.shape
    per = wide // HD
    tokens = 2 * width
    f_at, r_at, h_at = (lax.axis_index(a) for a in ("frame", "row", "head"))
    frame_id = [(f_at - 1, r_at, h_at), (f_at + 1, r_at, h_at)]
    row_id = [(f_at, r_at - 1, h_at), (f_at, r_at + 1, h_at)]
    head_id = (f_at, r_at, 1 - h_at)
    has_f = [f_at > 0, f_at < frames - 1]
    has_r = [r_at > 0, r_at < rows - 1]

    barrier = pltpu.get_barrier_semaphore()
    pl.semaphore_signal(barrier, inc=1, device_id=head_id, device_id_type=MESH)
    for s in (0, 1):
        for has, ids in ((has_f, frame_id), (has_r, row_id)):

            @pl.when(has[s])
            def _():
                pl.semaphore_signal(barrier, inc=1, device_id=ids[s], device_id_type=MESH)

    def remote(src, dst, send, recv, device):
        return pltpu.make_async_remote_copy(
            src_ref=src, dst_ref=dst, send_sem=send, recv_sem=recv,
            device_id=device, device_id_type=MESH,
        )

    def row_out(c, a, s):
        return remote(kv.at[c, a, 1, 1 + s], kv.at[c, a, 1, 3 - 3 * s],
                      row_s.at[c, a, s], row_r.at[c, a, 1 - s], row_id[s])

    def row_in(c, a, s):
        return remote(kv.at[c, a, 1, 1 + s], kv.at[c, a, 1, 3 * s],
                      row_s.at[c, a, s], row_r.at[c, a, s], row_id[s])

    def frame_out(c, a, s):
        return remote(kv.at[c, a, 1, pl.ds(1, 2)], kv.at[c, a, 2 - 2 * s, pl.ds(1, 2)],
                      fr_s.at[c, a, s], fr_r.at[c, a, 1 - s], frame_id[s])

    def frame_in(c, a, s):
        return remote(kv.at[c, a, 1, pl.ds(1, 2)], kv.at[c, a, 2 * s, pl.ds(1, 2)],
                      fr_s.at[c, a, s], fr_r.at[c, a, s], frame_id[s])

    def corner_out(c, a, s, t):
        return remote(kv.at[c, a, 1, 3 * t], kv.at[c, a, 2 - 2 * s, 3 * t],
                      co_s.at[c, a, s, t], co_r.at[c, a, 1 - s, t], frame_id[s])

    def corner_in(c, a, s, t):
        return remote(kv.at[c, a, 1, 3 * t], kv.at[c, a, 2 * s, 3 * t],
                      co_s.at[c, a, s, t], co_r.at[c, a, s, t], frame_id[s])

    def gx_copy(c, s, mine):
        return remote(gx_out.at[c, s], gx_in.at[c, s if mine else 1 - s],
                      gx_s.at[c, s], gx_r.at[c, s if mine else 1 - s], frame_id[s])

    def gy_copy(c, s, mine):
        return remote(gy_out.at[c, s], gy_in.at[c, s if mine else 1 - s],
                      gy_s.at[c, s], gy_r.at[c, s if mine else 1 - s], row_id[s])

    def hx_copy(i):
        return remote(hx_out.at[i], hx_in.at[i], hx_s.at[i], hx_r.at[i], head_id)

    def lanes(c):
        return slice(c * wide, (c + 1) * wide)

    for c in range(chunks):
        kv[c, 1, 1, 1:3] = v_ref[0, :, :, lanes(c)]
    for s in (0, 1):

        @pl.when(jnp.logical_not(has_f[s]))
        def _():
            def body(c, carry):
                kv[c, :, 2 * s] = jnp.zeros((2, 4, width, wide), BF16)
                gx_in[c, s] = jnp.zeros((2, 4, width, wide), BF16)
                return carry

            lax.fori_loop(0, chunks, body, 0)

        @pl.when(jnp.logical_not(has_r[s]))
        def _():
            def body(c, carry):
                for a in (0, 1):
                    for d in range(3):
                        kv[c, a, d, 3 * s] = jnp.zeros((width, wide), BF16)
                gy_in[c, s] = jnp.zeros((2, width, wide), BF16)
                return carry

            lax.fori_loop(0, chunks, body, 0)

    square_q = jnp.zeros((tokens, 128), F32)
    square_k = jnp.zeros((tokens, 128), F32)
    for i in range(chunks * per):
        part = slice(i * HD, (i + 1) * HD)
        q_part = q_ref[0, :, :, part].reshape(tokens, HD).astype(F32)
        k_part = k_ref[0, :, :, part].reshape(tokens, HD).astype(F32)
        square_q += q_part * q_part
        square_k += k_part * k_part
    hx_out[0] = columns_to_rows(
        jnp.sum(square_q, -1, keepdims=True), jnp.sum(square_k, -1, keepdims=True)
    )

    peers = 1
    for edge in (*has_f, *has_r):
        peers = peers + edge.astype(jnp.int32)
    pl.semaphore_wait(barrier, peers)

    hx_copy(0).start()

    def send_own(c, a):
        for s in (0, 1):

            @pl.when(has_r[s])
            def _():
                row_out(c, a, s).start()

            @pl.when(has_f[s])
            def _():
                frame_out(c, a, s).start()

    def v_body(c, carry):
        send_own(c, 1)
        return carry

    lax.fori_loop(0, chunks, v_body, 0)

    keys = 12 * width
    key = lax.broadcasted_iota(jnp.int32, (1, keys), 1)
    key_line = key // TC
    kept_row = jnp.zeros((1, keys), jnp.int32)
    for d in range(3):
        frame = f_at + (d - 1)
        frame_ok = jnp.logical_and(frame >= 0, frame < frames)
        for g in range(4):
            row = 2 * r_at + (g - 1)
            ok = jnp.logical_and(frame_ok, jnp.logical_and(row >= 0, row < 2 * rows))
            for tile in range(TILES):
                one = kept_ref[jnp.clip(frame, 0, frames - 1), jnp.clip(row, 0, 2 * rows - 1), tile]
                one = jnp.where(ok, one, 0)
                kept_row = jnp.where(key_line == (d * 4 + g) * TILES + tile, one, kept_row)
    query = lax.broadcasted_iota(jnp.int32, (tokens, keys), 0)
    keyb = lax.broadcasted_iota(jnp.int32, (tokens, keys), 1)
    q_row, q_tile = query // width + 1, (query % width) // TC
    k_line, k_tile = keyb // width, (keyb % width) // TC
    k_row = k_line % 4
    near = (jnp.abs(q_row - k_row) <= 1) & (jnp.abs(q_tile - k_tile) <= 1)
    same = (k_line == q_row + 4) & (q_tile == k_tile)
    kept_full = jnp.broadcast_to(kept_row, (tokens, keys)) > 0
    bias[...] = jnp.where(near & (kept_full | same), 0.0, NEG)

    hx_copy(0).wait()
    scale_q, scale_k = rows_to_columns(
        lax.rsqrt((hx_out[0] + hx_in[0]) / features + norm_eps)
    )
    for c in range(chunks):
        k_norm = k_ref[0, :, :, lanes(c)].reshape(tokens, wide).astype(F32) * scale_k
        k_norm = (k_norm * gk_ref[:, lanes(c)]).astype(BF16)
        kv[c, 0, 1, 1:3] = k_norm.reshape(2, width, wide)
        send_own(c, 0)
    for c in range(chunks):
        q_norm = q_ref[0, :, :, lanes(c)].reshape(tokens, wide).astype(F32) * scale_q
        qn[c] = (q_norm * gq_ref[:, lanes(c)]).astype(BF16)

    for a in (1, 0):

        def relay(c, carry, a=a):
            for t in (0, 1):

                @pl.when(has_r[t])
                def _():
                    row_in(c, a, t).wait_recv()

                for s in (0, 1):

                    @pl.when(jnp.logical_and(has_r[t], has_f[s]))
                    def _():
                        corner_out(c, a, s, t).start()

            return carry

        lax.fori_loop(0, chunks, relay, 0)

    acc[...] = jnp.zeros_like(acc)

    def finish_x(c):
        for s in (0, 1):

            @pl.when(has_f[s])
            def _():
                gx_copy(c, s, True).wait_recv()

        for a in (0, 1):
            for g in range(4):
                total = own[c, a, g] + gx_in[c, 0, a, g].astype(F32) + gx_in[c, 1, a, g].astype(F32)
                if g in (0, 3):
                    gy_out[c, g // 3, a] = total.astype(BF16)
                else:
                    own[c, a, g] = total
        for s in (0, 1):

            @pl.when(has_r[s])
            def _():
                gy_copy(c, s, False).start()

    def compute(c, carry):
        for s in (0, 1):

            @pl.when(has_f[s])
            def _():
                for a in (0, 1):
                    frame_in(c, a, s).wait_recv()

            for t in (0, 1):

                @pl.when(jnp.logical_and(has_r[t], has_f[s]))
                def _():
                    for a in (0, 1):
                        corner_in(c, a, s, t).wait_recv()

        for j in range(per):
            part = slice(j * HD, (j + 1) * HD)
            at = pl.ds(pl.multiple_of(c * wide + j * HD, HD), HD)
            query_h = qn[c, :, part]
            key_h = kv[c, 0, :, :, :, part].reshape(keys, HD)
            value_h = kv[c, 1, :, :, :, part].reshape(keys, HD)
            scores = dot(query_h, key_h, COLS_T) * (SCORE_SCALE * LOG2E) + bias[...]
            expo = jnp.exp2(scores - jnp.max(scores, -1, keepdims=True))
            prob = expo * (1.0 / jnp.sum(expo, -1, keepdims=True))
            prob_b = prob.astype(BF16)
            attended = dot(prob_b, value_h, PLAIN)
            target = t_ref[0, :, :, at].reshape(tokens, HD).astype(F32)
            d_out = (attended - target).astype(BF16)
            delta = jnp.sum(d_out.astype(F32) * attended, -1, keepdims=True)
            prob_grad = dot(d_out, value_h, COLS_T)
            score_grad = (prob * ((prob_grad - delta) * SCORE_SCALE)).astype(BF16)
            dq_h = dot(score_grad, key_h, PLAIN)
            gated = dq_h * gq_ref[:, at]
            dq[c, :, part] = gated
            acc[0] += gated * q_ref[0, :, :, at].reshape(tokens, HD).astype(F32)
            for a, grad in (
                (0, dot(score_grad, query_h, ROWS_T)),
                (1, dot(prob_b, d_out, ROWS_T)),
            ):
                grad = grad.reshape(3, 4, width, HD)
                own[c, a, :, :, part] = grad[1]
                for s in (0, 1):
                    gx_out[c, s, a, :, :, part] = grad[2 * s].astype(BF16)
        for s in (0, 1):

            @pl.when(has_f[s])
            def _():
                gx_copy(c, s, False).start()

        @pl.when(c >= 2)
        def _():
            finish_x(c - 2)

        return carry

    lax.fori_loop(0, chunks, compute, 0)

    def last_x(c, carry):
        finish_x(c)
        return carry

    lax.fori_loop(max(chunks - 2, 0), chunks, last_x, 0)

    def finish_y(c, carry):
        at = pl.ds(pl.multiple_of(c * wide, HD), wide)
        for s in (0, 1):

            @pl.when(has_r[s])
            def _():
                gy_copy(c, s, True).wait_recv()

        ov_ref[0, :, :, at] = (own[c, 1, 1:3] + gy_in[c, :, 1].astype(F32)).astype(BF16)
        gated = (own[c, 0, 1:3] + gy_in[c, :, 0].astype(F32)).reshape(tokens, wide) * gk_ref[:, at]
        own[c, 0, 1:3] = gated.reshape(2, width, wide)
        product = gated * k_ref[0, :, :, at].reshape(tokens, wide).astype(F32)
        for j in range(per):
            acc[1] += product[:, j * HD : (j + 1) * HD]
        return carry

    lax.fori_loop(0, chunks, finish_y, 0)

    hx_out[1] = columns_to_rows(
        jnp.sum(acc[0], -1, keepdims=True), jnp.sum(acc[1], -1, keepdims=True)
    )
    hx_copy(1).start()
    hx_copy(1).wait()
    sum_q, sum_k = rows_to_columns((hx_out[1] + hx_in[1]) / features)
    back_q = scale_q * scale_q * scale_q * sum_q
    back_k = scale_k * scale_k * scale_k * sum_k
    for c in range(chunks):
        q_float = q_ref[0, :, :, lanes(c)].reshape(tokens, wide).astype(F32)
        grad_q = scale_q * dq[c] - q_float * back_q
        oq_ref[0, :, :, lanes(c)] = grad_q.astype(BF16).reshape(2, width, wide)
        k_float = k_ref[0, :, :, lanes(c)].reshape(tokens, wide).astype(F32)
        grad_k = scale_k * own[c, 0, 1:3].reshape(tokens, wide) - k_float * back_k
        ok_ref[0, :, :, lanes(c)] = grad_k.astype(BF16).reshape(2, width, wide)

    def drain(c, carry):
        for s in (0, 1):

            @pl.when(has_r[s])
            def _():
                for a in (0, 1):
                    row_out(c, a, s).wait_send()
                gy_copy(c, s, False).wait_send()

            @pl.when(has_f[s])
            def _():
                for a in (0, 1):
                    frame_out(c, a, s).wait_send()
                gx_copy(c, s, False).wait_send()

            for t in (0, 1):

                @pl.when(jnp.logical_and(has_r[t], has_f[s]))
                def _():
                    for a in (0, 1):
                        corner_out(c, a, s, t).wait_send()

        return carry

    lax.fori_loop(0, chunks, drain, 0)


def per_device(sizes, per, q_pre, k_pre, values, target, gain_q, gain_k, kept):
    _, _, width, feat_dev = q_pre.shape
    chunks, wide = feat_dev // (per * HD), per * HD
    dma = pltpu.SemaphoreType.DMA
    vmem = pl.BlockSpec(memory_space=pltpu.VMEM)
    out = jax.ShapeDtypeStruct(q_pre.shape, BF16)
    return pl.pallas_call(
        functools.partial(kernel, sizes, feat_dev * sizes[2]),
        out_shape=(out, out, out),
        in_specs=[vmem] * 6 + [pl.BlockSpec(memory_space=pltpu.SMEM)],
        out_specs=(vmem, vmem, vmem),
        scratch_shapes=[
            pltpu.VMEM((chunks, 2, 3, 4, width, wide), BF16),
            pltpu.VMEM((chunks, 2 * width, wide), BF16),
            pltpu.VMEM((2 * width, 12 * width), F32),
            pltpu.VMEM((chunks, 2, 2, 4, width, wide), BF16),
            pltpu.VMEM((chunks, 2, 2, 4, width, wide), BF16),
            pltpu.VMEM((chunks, 2, 2, width, wide), BF16),
            pltpu.VMEM((chunks, 2, 2, width, wide), BF16),
            pltpu.VMEM((chunks, 2, 4, width, wide), F32),
            pltpu.VMEM((chunks, 2 * width, wide), F32),
            pltpu.VMEM((2, 2 * width, HD), F32),
            pltpu.VMEM((2, 8, 128), F32),
            pltpu.VMEM((2, 8, 128), F32),
            dma((chunks, 2, 2)),
            dma((chunks, 2, 2)),
            dma((chunks, 2, 2)),
            dma((chunks, 2, 2)),
            dma((chunks, 2, 2, 2)),
            dma((chunks, 2, 2, 2)),
            dma((chunks, 2)),
            dma((chunks, 2)),
            dma((chunks, 2)),
            dma((chunks, 2)),
            dma((2,)),
            dma((2,)),
        ],
        compiler_params=pltpu.CompilerParams(collective_id=0, has_side_effects=True),
    )(q_pre, k_pre, values, target, gain_q[None], gain_k[None], kept)


def solution(mesh):
    sizes = tuple(mesh.shape[a] for a in ("frame", "row", "head"))
    grid = P("frame", "row", None, "head")
    return jax.shard_map(
        functools.partial(per_device, sizes, 2),
        mesh=mesh,
        in_specs=(grid, grid, grid, grid, P("head"), P("head"), P()),
        out_specs=(grid, grid, grid),
        check_vma=False,
    )
```

```python
import functools

import jax
import jax.numpy as jnp
from jax import lax
from jax.experimental import pallas as pl
from jax.experimental.pallas import tpu as pltpu
from jax.sharding import PartitionSpec as P

TC = 16
HD = 128
TILES = 4
MESH = pl.DeviceIdType.MESH
norm_eps = 1e-06
LOG2E = 1.4426950408889634
SCORE_SCALE = HD ** (-0.5)
NEG = -1e30

BF16 = jnp.bfloat16
F32 = jnp.float32
ROWS_T = (((0,), (0,)), ((), ()))
COLS_T = (((1,), (1,)), ((), ()))
PLAIN = (((1,), (0,)), ((), ()))


def dot(a, b, dims):
    return lax.dot_general(a, b, dims, preferred_element_type=F32)


def columns_to_rows(col_a, col_b):
    lane = lax.broadcasted_iota(jnp.int32, (128, 128), 1)
    both = jnp.where(lane < 4, jnp.broadcast_to(col_a, (128, 128)), jnp.broadcast_to(col_b, (128, 128)))
    return both.T[0:8]


def rows_to_columns(rows):
    sub = lax.broadcasted_iota(jnp.int32, (128, 128), 0)
    both = jnp.where(
        sub < 64,
        jnp.broadcast_to(rows[0:1], (128, 128)),
        jnp.broadcast_to(rows[4:5], (128, 128)),
    ).T
    return both[:, 0:1], both[:, 64:65]


def kernel(
    sizes, features, q_hbm, k_hbm, v_hbm, t_hbm, gq_hbm, gk_hbm, kept_hbm,
    oq_ref, ok_ref, ov_ref,
    kv, qn, bias, gx_out, gx_in, gy_out, gy_in, own, dq, acc, hx_out, hx_in,
    row_s, row_r, fr_s, fr_r, co_s, co_r, gx_s, gx_r, gy_s, gy_r, hx_s, hx_r,
    q_ref, k_ref, v_ref, t_ref, gq_ref, gk_ref, kept_ref, load_s,
):
    frames, rows, heads = sizes
    chunks, _, _, _, width, wide = kv.shape
    per = wide // HD
    tokens = 2 * width
    f_at, r_at, h_at = (lax.axis_index(a) for a in ("frame", "row", "head"))
    frame_id = [(f_at - 1, r_at, h_at), (f_at + 1, r_at, h_at)]
    row_id = [(f_at, r_at - 1, h_at), (f_at, r_at + 1, h_at)]
    head_id = (f_at, r_at, 1 - h_at)
    has_f = [f_at > 0, f_at < frames - 1]
    has_r = [r_at > 0, r_at < rows - 1]

    loads = [
        pltpu.make_async_copy(src, dst, load_s.at[i])
        for i, (src, dst) in enumerate(
            (
                (q_hbm, q_ref), (k_hbm, k_ref), (v_hbm, v_ref), (kept_hbm, kept_ref),
                (gk_hbm, gk_ref.at[0]), (gq_hbm, gq_ref.at[0]), (t_hbm, t_ref),
            )
        )
    ]
    for load in loads:
        load.start()
    barrier = pltpu.get_barrier_semaphore()
    pl.semaphore_signal(barrier, inc=1, device_id=head_id, device_id_type=MESH)
    for s in (0, 1):
        for has, ids in ((has_f, frame_id), (has_r, row_id)):

            @pl.when(has[s])
            def _():
                pl.semaphore_signal(barrier, inc=1, device_id=ids[s], device_id_type=MESH)

    def remote(src, dst, send, recv, device):
        return pltpu.make_async_remote_copy(
            src_ref=src, dst_ref=dst, send_sem=send, recv_sem=recv,
            device_id=device, device_id_type=MESH,
        )

    def row_out(c, a, s):
        return remote(kv.at[c, a, 1, 1 + s], kv.at[c, a, 1, 3 - 3 * s],
                      row_s.at[c, a, s], row_r.at[c, a, 1 - s], row_id[s])

    def row_in(c, a, s):
        return remote(kv.at[c, a, 1, 1 + s], kv.at[c, a, 1, 3 * s],
                      row_s.at[c, a, s], row_r.at[c, a, s], row_id[s])

    def frame_out(c, a, s):
        return remote(kv.at[c, a, 1, pl.ds(1, 2)], kv.at[c, a, 2 - 2 * s, pl.ds(1, 2)],
                      fr_s.at[c, a, s], fr_r.at[c, a, 1 - s], frame_id[s])

    def frame_in(c, a, s):
        return remote(kv.at[c, a, 1, pl.ds(1, 2)], kv.at[c, a, 2 * s, pl.ds(1, 2)],
                      fr_s.at[c, a, s], fr_r.at[c, a, s], frame_id[s])

    def corner_out(c, a, s, t):
        return remote(kv.at[c, a, 1, 3 * t], kv.at[c, a, 2 - 2 * s, 3 * t],
                      co_s.at[c, a, s, t], co_r.at[c, a, 1 - s, t], frame_id[s])

    def corner_in(c, a, s, t):
        return remote(kv.at[c, a, 1, 3 * t], kv.at[c, a, 2 * s, 3 * t],
                      co_s.at[c, a, s, t], co_r.at[c, a, s, t], frame_id[s])

    def gx_copy(c, s, mine):
        return remote(gx_out.at[c, s], gx_in.at[c, s if mine else 1 - s],
                      gx_s.at[c, s], gx_r.at[c, s if mine else 1 - s], frame_id[s])

    def gy_copy(c, s, mine):
        return remote(gy_out.at[c, s], gy_in.at[c, s if mine else 1 - s],
                      gy_s.at[c, s], gy_r.at[c, s if mine else 1 - s], row_id[s])

    def hx_copy(i):
        return remote(hx_out.at[i], hx_in.at[i], hx_s.at[i], hx_r.at[i], head_id)

    def lanes(c):
        return slice(c * wide, (c + 1) * wide)

    for s in (0, 1):

        @pl.when(jnp.logical_not(has_f[s]))
        def _():
            def body(c, carry):
                kv[c, :, 2 * s] = jnp.zeros((2, 4, width, wide), BF16)
                gx_in[c, s] = jnp.zeros((2, 4, width, wide), BF16)
                return carry

            lax.fori_loop(0, chunks, body, 0)

        @pl.when(jnp.logical_not(has_r[s]))
        def _():
            def body(c, carry):
                for a in (0, 1):
                    for d in range(3):
                        kv[c, a, d, 3 * s] = jnp.zeros((width, wide), BF16)
                gy_in[c, s] = jnp.zeros((2, width, wide), BF16)
                return carry

            lax.fori_loop(0, chunks, body, 0)

    loads[0].wait()
    loads[1].wait()
    square_q = jnp.zeros((tokens, 128), F32)
    square_k = jnp.zeros((tokens, 128), F32)
    for i in range(chunks * per):
        part = slice(i * HD, (i + 1) * HD)
        q_part = q_ref[0, :, :, part].reshape(tokens, HD).astype(F32)
        k_part = k_ref[0, :, :, part].reshape(tokens, HD).astype(F32)
        square_q += q_part * q_part
        square_k += k_part * k_part
    hx_out[0] = columns_to_rows(
        jnp.sum(square_q, -1, keepdims=True), jnp.sum(square_k, -1, keepdims=True)
    )

    loads[2].wait()
    for c in range(chunks):
        kv[c, 1, 1, 1:3] = v_ref[0, :, :, lanes(c)]
    peers = 1
    for edge in (*has_f, *has_r):
        peers = peers + edge.astype(jnp.int32)
    pl.semaphore_wait(barrier, peers)

    hx_copy(0).start()

    def send_own(c, a):
        for s in (0, 1):

            @pl.when(has_r[s])
            def _():
                row_out(c, a, s).start()

            @pl.when(has_f[s])
            def _():
                frame_out(c, a, s).start()

    def v_body(c, carry):
        send_own(c, 1)
        return carry

    lax.fori_loop(0, chunks, v_body, 0)

    loads[3].wait()
    keys = 12 * width
    key = lax.broadcasted_iota(jnp.int32, (1, keys), 1)
    key_line = key // TC
    kept_row = jnp.zeros((1, keys), jnp.int32)
    for d in range(3):
        frame = f_at + (d - 1)
        frame_ok = jnp.logical_and(frame >= 0, frame < frames)
        for g in range(4):
            row = 2 * r_at + (g - 1)
            ok = jnp.logical_and(frame_ok, jnp.logical_and(row >= 0, row < 2 * rows))
            for tile in range(TILES):
                one = kept_ref[jnp.clip(frame, 0, frames - 1), tile, jnp.clip(row, 0, 2 * rows - 1)]
                one = jnp.where(ok, one, 0)
                kept_row = jnp.where(key_line == (d * 4 + g) * TILES + tile, one, kept_row)
    query = lax.broadcasted_iota(jnp.int32, (tokens, keys), 0)
    keyb = lax.broadcasted_iota(jnp.int32, (tokens, keys), 1)
    q_row, q_tile = query // width + 1, (query % width) // TC
    k_line, k_tile = keyb // width, (keyb % width) // TC
    k_row = k_line % 4
    near = (jnp.abs(q_row - k_row) <= 1) & (jnp.abs(q_tile - k_tile) <= 1)
    same = (k_line == q_row + 4) & (q_tile == k_tile)
    kept_full = jnp.broadcast_to(kept_row, (tokens, keys)) > 0
    bias[...] = jnp.where(near & (kept_full | same), 0.0, NEG)

    for load in loads[4:]:
        load.wait()
    hx_copy(0).wait()
    scale_q, scale_k = rows_to_columns(
        lax.rsqrt((hx_out[0] + hx_in[0]) / features + norm_eps)
    )
    for c in range(chunks):
        k_norm = k_ref[0, :, :, lanes(c)].reshape(tokens, wide).astype(F32) * scale_k
        k_norm = (k_norm * gk_ref[:, lanes(c)]).astype(BF16)
        kv[c, 0, 1, 1:3] = k_norm.reshape(2, width, wide)
        send_own(c, 0)
    for c in range(chunks):
        q_norm = q_ref[0, :, :, lanes(c)].reshape(tokens, wide).astype(F32) * scale_q
        qn[c] = (q_norm * gq_ref[:, lanes(c)]).astype(BF16)

    for a in (1, 0):

        def relay(c, carry, a=a):
            for t in (0, 1):

                @pl.when(has_r[t])
                def _():
                    row_in(c, a, t).wait_recv()

                for s in (0, 1):

                    @pl.when(jnp.logical_and(has_r[t], has_f[s]))
                    def _():
                        corner_out(c, a, s, t).start()

            return carry

        lax.fori_loop(0, chunks, relay, 0)

    acc[...] = jnp.zeros_like(acc)

    def finish_x(c):
        for s in (0, 1):

            @pl.when(has_f[s])
            def _():
                gx_copy(c, s, True).wait_recv()

        for a in (0, 1):
            for g in range(4):
                total = own[c, a, g] + gx_in[c, 0, a, g].astype(F32) + gx_in[c, 1, a, g].astype(F32)
                if g in (0, 3):
                    gy_out[c, g // 3, a] = total.astype(BF16)
                else:
                    own[c, a, g] = total
        for s in (0, 1):

            @pl.when(has_r[s])
            def _():
                gy_copy(c, s, False).start()

    def compute(c, carry):
        for s in (0, 1):

            @pl.when(has_f[s])
            def _():
                for a in (0, 1):
                    frame_in(c, a, s).wait_recv()

            for t in (0, 1):

                @pl.when(jnp.logical_and(has_r[t], has_f[s]))
                def _():
                    for a in (0, 1):
                        corner_in(c, a, s, t).wait_recv()

        for j in range(per):
            part = slice(j * HD, (j + 1) * HD)
            at = pl.ds(pl.multiple_of(c * wide + j * HD, HD), HD)
            query_h = qn[c, :, part]
            key_h = kv[c, 0, :, :, :, part].reshape(keys, HD)
            value_h = kv[c, 1, :, :, :, part].reshape(keys, HD)
            scores = dot(query_h, key_h, COLS_T) * (SCORE_SCALE * LOG2E) + bias[...]
            expo = jnp.exp2(scores - jnp.max(scores, -1, keepdims=True))
            prob = expo * (1.0 / jnp.sum(expo, -1, keepdims=True))
            prob_b = prob.astype(BF16)
            attended = dot(prob_b, value_h, PLAIN)
            target = t_ref[0, :, :, at].reshape(tokens, HD).astype(F32)
            d_out = (attended - target).astype(BF16)
            delta = jnp.sum(d_out.astype(F32) * attended, -1, keepdims=True)
            prob_grad = dot(d_out, value_h, COLS_T)
            score_grad = (prob * ((prob_grad - delta) * SCORE_SCALE)).astype(BF16)
            dq_h = dot(score_grad, key_h, PLAIN)
            gated = dq_h * gq_ref[:, at]
            dq[c, :, part] = gated
            acc[0] += gated * q_ref[0, :, :, at].reshape(tokens, HD).astype(F32)
            for a, grad in (
                (0, dot(score_grad, query_h, ROWS_T)),
                (1, dot(prob_b, d_out, ROWS_T)),
            ):
                grad = grad.reshape(3, 4, width, HD)
                own[c, a, :, :, part] = grad[1]
                for s in (0, 1):
                    gx_out[c, s, a, :, :, part] = grad[2 * s].astype(BF16)
        for s in (0, 1):

            @pl.when(has_f[s])
            def _():
                gx_copy(c, s, False).start()

        @pl.when(c >= 2)
        def _():
            finish_x(c - 2)

        return carry

    lax.fori_loop(0, chunks, compute, 0)

    def last_x(c, carry):
        finish_x(c)
        return carry

    lax.fori_loop(max(chunks - 2, 0), chunks, last_x, 0)

    def finish_y(c, carry):
        at = pl.ds(pl.multiple_of(c * wide, HD), wide)
        for s in (0, 1):

            @pl.when(has_r[s])
            def _():
                gy_copy(c, s, True).wait_recv()

        ov_ref[0, :, :, at] = (own[c, 1, 1:3] + gy_in[c, :, 1].astype(F32)).astype(BF16)
        gated = (own[c, 0, 1:3] + gy_in[c, :, 0].astype(F32)).reshape(tokens, wide) * gk_ref[:, at]
        own[c, 0, 1:3] = gated.reshape(2, width, wide)
        product = gated * k_ref[0, :, :, at].reshape(tokens, wide).astype(F32)
        for j in range(per):
            acc[1] += product[:, j * HD : (j + 1) * HD]
        return carry

    lax.fori_loop(0, chunks, finish_y, 0)

    hx_out[1] = columns_to_rows(
        jnp.sum(acc[0], -1, keepdims=True), jnp.sum(acc[1], -1, keepdims=True)
    )
    hx_copy(1).start()
    hx_copy(1).wait()
    sum_q, sum_k = rows_to_columns((hx_out[1] + hx_in[1]) / features)
    back_q = scale_q * scale_q * scale_q * sum_q
    back_k = scale_k * scale_k * scale_k * sum_k
    for c in range(chunks):
        q_float = q_ref[0, :, :, lanes(c)].reshape(tokens, wide).astype(F32)
        grad_q = scale_q * dq[c] - q_float * back_q
        oq_ref[0, :, :, lanes(c)] = grad_q.astype(BF16).reshape(2, width, wide)
        k_float = k_ref[0, :, :, lanes(c)].reshape(tokens, wide).astype(F32)
        grad_k = scale_k * own[c, 0, 1:3].reshape(tokens, wide) - k_float * back_k
        ok_ref[0, :, :, lanes(c)] = grad_k.astype(BF16).reshape(2, width, wide)

    def drain(c, carry):
        for s in (0, 1):

            @pl.when(has_r[s])
            def _():
                for a in (0, 1):
                    row_out(c, a, s).wait_send()
                gy_copy(c, s, False).wait_send()

            @pl.when(has_f[s])
            def _():
                for a in (0, 1):
                    frame_out(c, a, s).wait_send()
                gx_copy(c, s, False).wait_send()

            for t in (0, 1):

                @pl.when(jnp.logical_and(has_r[t], has_f[s]))
                def _():
                    for a in (0, 1):
                        corner_out(c, a, s, t).wait_send()

        return carry

    lax.fori_loop(0, chunks, drain, 0)


def per_device(sizes, per, q_pre, k_pre, values, target, gain_q, gain_k, kept):
    _, _, width, feat_dev = q_pre.shape
    chunks, wide = feat_dev // (per * HD), per * HD
    dma = pltpu.SemaphoreType.DMA
    vmem = pl.BlockSpec(memory_space=pltpu.VMEM)
    out = jax.ShapeDtypeStruct(q_pre.shape, BF16)
    return pl.pallas_call(
        functools.partial(kernel, sizes, feat_dev * sizes[2]),
        out_shape=(out, out, out),
        in_specs=[pl.BlockSpec(memory_space=pltpu.HBM)] * 7,
        out_specs=(vmem, vmem, vmem),
        scratch_shapes=[
            pltpu.VMEM((chunks, 2, 3, 4, width, wide), BF16),
            pltpu.VMEM((chunks, 2 * width, wide), BF16),
            pltpu.VMEM((2 * width, 12 * width), F32),
            pltpu.VMEM((chunks, 2, 2, 4, width, wide), BF16),
            pltpu.VMEM((chunks, 2, 2, 4, width, wide), BF16),
            pltpu.VMEM((chunks, 2, 2, width, wide), BF16),
            pltpu.VMEM((chunks, 2, 2, width, wide), BF16),
            pltpu.VMEM((chunks, 2, 4, width, wide), F32),
            pltpu.VMEM((chunks, 2 * width, wide), F32),
            pltpu.VMEM((2, 2 * width, HD), F32),
            pltpu.VMEM((2, 8, 128), F32),
            pltpu.VMEM((2, 8, 128), F32),
            dma((chunks, 2, 2)),
            dma((chunks, 2, 2)),
            dma((chunks, 2, 2)),
            dma((chunks, 2, 2)),
            dma((chunks, 2, 2, 2)),
            dma((chunks, 2, 2, 2)),
            dma((chunks, 2)),
            dma((chunks, 2)),
            dma((chunks, 2)),
            dma((chunks, 2)),
            dma((2,)),
            dma((2,)),
            *([pltpu.VMEM(q_pre.shape, BF16)] * 4),
            pltpu.VMEM((1, feat_dev), F32),
            pltpu.VMEM((1, feat_dev), F32),
            pltpu.SMEM((kept.shape[0], TILES, kept.shape[1]), jnp.int32),
            dma((7,)),
        ],
        compiler_params=pltpu.CompilerParams(vmem_limit_bytes=60 << 20, collective_id=0, has_side_effects=True),
    )(q_pre, k_pre, values, target, gain_q, gain_k, kept.transpose(0, 2, 1))


def solution(mesh):
    sizes = tuple(mesh.shape[a] for a in ("frame", "row", "head"))
    grid = P("frame", "row", None, "head")
    return jax.shard_map(
        functools.partial(per_device, sizes, 2),
        mesh=mesh,
        in_specs=(grid, grid, grid, grid, P("head"), P("head"), P()),
        out_specs=(grid, grid, grid),
        check_vma=False,
    )
```

```python
import functools

import jax
import jax.numpy as jnp
from jax import lax
from jax.experimental import pallas as pl
from jax.experimental.pallas import tpu as pltpu
from jax.sharding import PartitionSpec as P

TC = 16
HD = 128
TILES = 4
MESH = pl.DeviceIdType.MESH
norm_eps = 1e-06
LOG2E = 1.4426950408889634
SCORE_SCALE = HD ** (-0.5)
NEG = -1e30

BF16 = jnp.bfloat16
F32 = jnp.float32
ROWS_T = (((0,), (0,)), ((), ()))
COLS_T = (((1,), (1,)), ((), ()))
PLAIN = (((1,), (0,)), ((), ()))


def dot(a, b, dims):
    return lax.dot_general(a, b, dims, preferred_element_type=F32)


def columns_to_rows(col_a, col_b):
    lane = lax.broadcasted_iota(jnp.int32, (128, 128), 1)
    both = jnp.where(lane < 4, jnp.broadcast_to(col_a, (128, 128)), jnp.broadcast_to(col_b, (128, 128)))
    return both.T[0:8]


def rows_to_columns(rows):
    sub = lax.broadcasted_iota(jnp.int32, (128, 128), 0)
    both = jnp.where(
        sub < 64,
        jnp.broadcast_to(rows[0:1], (128, 128)),
        jnp.broadcast_to(rows[4:5], (128, 128)),
    ).T
    return both[:, 0:1], both[:, 64:65]


def kernel(
    sizes, features, q_hbm, k_hbm, v_hbm, t_hbm, gq_hbm, gk_hbm, kept_hbm,
    oq_ref, ok_ref, ov_ref,
    kv, qn, bias, gx_out, gx_in, gy_out, gy_in, own, dq, acc, hx_out, hx_in,
    row_s, row_r, fr_s, fr_r, co_s, co_r, gx_s, gx_r, gy_s, gy_r, hx_s, hx_r,
    q_ref, k_ref, v_ref, t_ref, gq_ref, gk_ref, kept_ref, load_s,
    w_out, w_in, wx_out, wx_in, wy_out, wy_in, w_s, w_r, wx_s, wx_r, wy_s, wy_r,
):
    frames, rows, heads = sizes
    chunks, _, _, _, width, wide = kv.shape
    per = wide // HD
    tokens = 2 * width
    f_at, r_at, h_at = (lax.axis_index(a) for a in ("frame", "row", "head"))
    frame_id = [(f_at - 1, r_at, h_at), (f_at + 1, r_at, h_at)]
    row_id = [(f_at, r_at - 1, h_at), (f_at, r_at + 1, h_at)]
    head_id = (f_at, r_at, 1 - h_at)
    has_f = [f_at > 0, f_at < frames - 1]
    has_r = [r_at > 0, r_at < rows - 1]

    loads = [
        pltpu.make_async_copy(src, dst, load_s.at[i])
        for i, (src, dst) in enumerate(
            (
                (q_hbm, q_ref), (k_hbm, k_ref), (v_hbm, v_ref), (kept_hbm, kept_ref),
                (gk_hbm, gk_ref.at[0]), (gq_hbm, gq_ref.at[0]), (t_hbm, t_ref),
            )
        )
    ]
    for load in loads:
        load.start()
    barrier = pltpu.get_barrier_semaphore()
    pl.semaphore_signal(barrier, inc=1, device_id=head_id, device_id_type=MESH)
    for s in (0, 1):
        for has, ids in ((has_f, frame_id), (has_r, row_id)):

            @pl.when(has[s])
            def _():
                pl.semaphore_signal(barrier, inc=1, device_id=ids[s], device_id_type=MESH)

    def remote(src, dst, send, recv, device):
        return pltpu.make_async_remote_copy(
            src_ref=src, dst_ref=dst, send_sem=send, recv_sem=recv,
            device_id=device, device_id_type=MESH,
        )

    def row_out(c, a, s):
        return remote(kv.at[c, a, 1, 1 + s], kv.at[c, a, 1, 3 - 3 * s],
                      row_s.at[c, a, s], row_r.at[c, a, 1 - s], row_id[s])

    def row_in(c, a, s):
        return remote(kv.at[c, a, 1, 1 + s], kv.at[c, a, 1, 3 * s],
                      row_s.at[c, a, s], row_r.at[c, a, s], row_id[s])

    def frame_out(c, a, s):
        return remote(kv.at[c, a, 1, pl.ds(1, 2)], kv.at[c, a, 2 - 2 * s, pl.ds(1, 2)],
                      fr_s.at[c, a, s], fr_r.at[c, a, 1 - s], frame_id[s])

    def frame_in(c, a, s):
        return remote(kv.at[c, a, 1, pl.ds(1, 2)], kv.at[c, a, 2 * s, pl.ds(1, 2)],
                      fr_s.at[c, a, s], fr_r.at[c, a, s], frame_id[s])

    def corner_out(c, a, s, t):
        return remote(kv.at[c, a, 1, 3 * t], kv.at[c, a, 2 - 2 * s, 3 * t],
                      co_s.at[c, a, s, t], co_r.at[c, a, 1 - s, t], frame_id[s])

    def corner_in(c, a, s, t):
        return remote(kv.at[c, a, 1, 3 * t], kv.at[c, a, 2 * s, 3 * t],
                      co_s.at[c, a, s, t], co_r.at[c, a, s, t], frame_id[s])

    def gx_copy(c, s, mine):
        return remote(gx_out.at[c, s], gx_in.at[c, s if mine else 1 - s],
                      gx_s.at[c, s], gx_r.at[c, s if mine else 1 - s], frame_id[s])

    def gy_copy(c, s, mine):
        return remote(gy_out.at[c, s], gy_in.at[c, s if mine else 1 - s],
                      gy_s.at[c, s], gy_r.at[c, s if mine else 1 - s], row_id[s])

    def w_copy():
        return remote(w_out, w_in, w_s.at[0], w_r.at[0], head_id)

    def wx_copy(s, mine):
        return remote(wx_out.at[s], wx_in.at[s if mine else 1 - s],
                      wx_s.at[s], wx_r.at[s if mine else 1 - s], frame_id[s])

    def wy_copy(s, mine):
        return remote(wy_out.at[s], wy_in.at[s if mine else 1 - s],
                      wy_s.at[s], wy_r.at[s if mine else 1 - s], row_id[s])

    def hx_copy(i):
        return remote(hx_out.at[i], hx_in.at[i], hx_s.at[i], hx_r.at[i], head_id)

    def lanes(c):
        return slice(c * wide, (c + 1) * wide)

    for s in (0, 1):

        @pl.when(jnp.logical_not(has_f[s]))
        def _():
            wx_in[s] = jnp.zeros((1, 4 * width), F32)

            def body(c, carry):
                kv[c, :, 2 * s] = jnp.zeros((2, 4, width, wide), BF16)
                gx_in[c, s] = jnp.zeros((2, 4, width, wide), BF16)
                return carry

            lax.fori_loop(0, chunks, body, 0)

        @pl.when(jnp.logical_not(has_r[s]))
        def _():
            wy_in[s] = jnp.zeros((1, 2 * width), F32)

            def body(c, carry):
                for a in (0, 1):
                    for d in range(3):
                        kv[c, a, d, 3 * s] = jnp.zeros((width, wide), BF16)
                gy_in[c, s] = jnp.zeros((2, width, wide), BF16)
                return carry

            lax.fori_loop(0, chunks, body, 0)

    loads[0].wait()
    loads[1].wait()
    square_q = jnp.zeros((tokens, 128), F32)
    square_k = jnp.zeros((tokens, 128), F32)
    for i in range(chunks * per):
        part = slice(i * HD, (i + 1) * HD)
        q_part = q_ref[0, :, :, part].reshape(tokens, HD).astype(F32)
        k_part = k_ref[0, :, :, part].reshape(tokens, HD).astype(F32)
        square_q += q_part * q_part
        square_k += k_part * k_part
    hx_out[0] = columns_to_rows(
        jnp.sum(square_q, -1, keepdims=True), jnp.sum(square_k, -1, keepdims=True)
    )

    loads[2].wait()
    for c in range(chunks):
        kv[c, 1, 1, 1:3] = v_ref[0, :, :, lanes(c)]
    peers = 1
    for edge in (*has_f, *has_r):
        peers = peers + edge.astype(jnp.int32)
    pl.semaphore_wait(barrier, peers)

    hx_copy(0).start()

    def send_own(c, a):
        for s in (0, 1):

            @pl.when(has_r[s])
            def _():
                row_out(c, a, s).start()

            @pl.when(has_f[s])
            def _():
                frame_out(c, a, s).start()

    def v_body(c, carry):
        send_own(c, 1)
        return carry

    lax.fori_loop(0, chunks, v_body, 0)

    loads[3].wait()
    keys = 12 * width
    key = lax.broadcasted_iota(jnp.int32, (1, keys), 1)
    key_line = key // TC
    kept_row = jnp.zeros((1, keys), jnp.int32)
    for d in range(3):
        frame = f_at + (d - 1)
        frame_ok = jnp.logical_and(frame >= 0, frame < frames)
        for g in range(4):
            row = 2 * r_at + (g - 1)
            ok = jnp.logical_and(frame_ok, jnp.logical_and(row >= 0, row < 2 * rows))
            for tile in range(TILES):
                one = kept_ref[jnp.clip(frame, 0, frames - 1), tile, jnp.clip(row, 0, 2 * rows - 1)]
                one = jnp.where(ok, one, 0)
                kept_row = jnp.where(key_line == (d * 4 + g) * TILES + tile, one, kept_row)
    query = lax.broadcasted_iota(jnp.int32, (tokens, keys), 0)
    keyb = lax.broadcasted_iota(jnp.int32, (tokens, keys), 1)
    q_row, q_tile = query // width + 1, (query % width) // TC
    k_line, k_tile = keyb // width, (keyb % width) // TC
    k_row = k_line % 4
    near = (jnp.abs(q_row - k_row) <= 1) & (jnp.abs(q_tile - k_tile) <= 1)
    same = (k_line == q_row + 4) & (q_tile == k_tile)
    kept_full = jnp.broadcast_to(kept_row, (tokens, keys)) > 0
    bias[...] = jnp.where(near & (kept_full | same), 0.0, NEG)

    for load in loads[4:]:
        load.wait()
    hx_copy(0).wait()
    scale_q, scale_k = rows_to_columns(
        lax.rsqrt((hx_out[0] + hx_in[0]) / features + norm_eps)
    )
    for c in range(chunks):
        k_norm = k_ref[0, :, :, lanes(c)].reshape(tokens, wide).astype(F32) * scale_k
        k_norm = (k_norm * gk_ref[:, lanes(c)]).astype(BF16)
        kv[c, 0, 1, 1:3] = k_norm.reshape(2, width, wide)
        send_own(c, 0)
    for c in range(chunks):
        q_norm = q_ref[0, :, :, lanes(c)].reshape(tokens, wide).astype(F32) * scale_q
        qn[c] = (q_norm * gq_ref[:, lanes(c)]).astype(BF16)

    for a in (1, 0):

        def relay(c, carry, a=a):
            for t in (0, 1):

                @pl.when(has_r[t])
                def _():
                    row_in(c, a, t).wait_recv()

                for s in (0, 1):

                    @pl.when(jnp.logical_and(has_r[t], has_f[s]))
                    def _():
                        corner_out(c, a, s, t).start()

            return carry

        lax.fori_loop(0, chunks, relay, 0)

    acc[...] = jnp.zeros_like(acc)
    w_out[...] = jnp.zeros_like(w_out)

    def finish_x(c):
        for s in (0, 1):

            @pl.when(has_f[s])
            def _():
                gx_copy(c, s, True).wait_recv()

        for a in (0, 1):
            for g in range(4):
                total = own[c, a, g] + gx_in[c, 0, a, g].astype(F32) + gx_in[c, 1, a, g].astype(F32)
                if g in (0, 3):
                    gy_out[c, g // 3, a] = total.astype(BF16)
                else:
                    own[c, a, g] = total
        for s in (0, 1):

            @pl.when(has_r[s])
            def _():
                gy_copy(c, s, False).start()

    def compute(c, carry):
        for s in (0, 1):

            @pl.when(has_f[s])
            def _():
                for a in (0, 1):
                    frame_in(c, a, s).wait_recv()

            for t in (0, 1):

                @pl.when(jnp.logical_and(has_r[t], has_f[s]))
                def _():
                    for a in (0, 1):
                        corner_in(c, a, s, t).wait_recv()

        for j in range(per):
            part = slice(j * HD, (j + 1) * HD)
            at = pl.ds(pl.multiple_of(c * wide + j * HD, HD), HD)
            query_h = qn[c, :, part]
            key_h = kv[c, 0, :, :, :, part].reshape(keys, HD)
            value_h = kv[c, 1, :, :, :, part].reshape(keys, HD)
            inner = dot(query_h, key_h, COLS_T)
            scores = inner * (SCORE_SCALE * LOG2E) + bias[...]
            expo = jnp.exp2(scores - jnp.max(scores, -1, keepdims=True))
            prob = expo * (1.0 / jnp.sum(expo, -1, keepdims=True))
            prob_b = prob.astype(BF16)
            attended = dot(prob_b, value_h, PLAIN)
            target = t_ref[0, :, :, at].reshape(tokens, HD).astype(F32)
            d_out = (attended - target).astype(BF16)
            delta = jnp.sum(d_out.astype(F32) * attended, -1, keepdims=True)
            prob_grad = dot(d_out, value_h, COLS_T)
            score_grad = (prob * ((prob_grad - delta) * SCORE_SCALE)).astype(BF16)
            w_out[...] += jnp.sum(score_grad.astype(F32) * inner, 0, keepdims=True)
            dq_h = dot(score_grad, key_h, PLAIN)
            gated = dq_h * gq_ref[:, at]
            dq[c, :, part] = gated
            acc[...] += gated * q_ref[0, :, :, at].reshape(tokens, HD).astype(F32)
            for a, grad in (
                (0, dot(score_grad, query_h, ROWS_T)),
                (1, dot(prob_b, d_out, ROWS_T)),
            ):
                grad = grad.reshape(3, 4, width, HD)
                own[c, a, :, :, part] = grad[1]
                for s in (0, 1):
                    gx_out[c, s, a, :, :, part] = grad[2 * s].astype(BF16)
        for s in (0, 1):

            @pl.when(has_f[s])
            def _():
                gx_copy(c, s, False).start()

        @pl.when(c >= 2)
        def _():
            finish_x(c - 2)

        return carry

    lax.fori_loop(0, chunks, compute, 0)

    sum_q = jnp.sum(acc[...], -1, keepdims=True)
    hx_out[1] = columns_to_rows(sum_q, sum_q)
    w_copy().start()
    hx_copy(1).start()
    w_copy().wait()
    both = w_out[...] + w_in[...]
    for s in (0, 1):
        wx_out[s] = both[:, 8 * s * width : (8 * s + 4) * width]

        @pl.when(has_f[s])
        def _():
            wx_copy(s, False).start()

    hx_copy(1).wait()
    sum_q, _ = rows_to_columns((hx_out[1] + hx_in[1]) / features)
    back_q = scale_q * scale_q * scale_q * sum_q
    for c in range(chunks):
        q_float = q_ref[0, :, :, lanes(c)].reshape(tokens, wide).astype(F32)
        grad_q = scale_q * dq[c] - q_float * back_q
        oq_ref[0, :, :, lanes(c)] = grad_q.astype(BF16).reshape(2, width, wide)

    def last_x(c, carry):
        finish_x(c)
        return carry

    lax.fori_loop(max(chunks - 2, 0), chunks, last_x, 0)

    for s in (0, 1):

        @pl.when(has_f[s])
        def _():
            wx_copy(s, True).wait_recv()

    mine = both[:, 4 * width : 8 * width] + wx_in[0] + wx_in[1]
    halves = [mine[:, 0 : 2 * width], mine[:, 2 * width : 4 * width]]
    for s in (0, 1):
        wy_out[s] = halves[s]

        @pl.when(has_r[s])
        def _():
            wy_copy(s, False).start()

    def finish_y(c, carry):
        at = pl.ds(pl.multiple_of(c * wide, HD), wide)
        for s in (0, 1):

            @pl.when(has_r[s])
            def _():
                gy_copy(c, s, True).wait_recv()

        ov_ref[0, :, :, at] = (own[c, 1, 1:3] + gy_in[c, :, 1].astype(F32)).astype(BF16)
        gated = (own[c, 0, 1:3] + gy_in[c, :, 0].astype(F32)).reshape(tokens, wide) * gk_ref[:, at]
        own[c, 0, 1:3] = (gated * scale_k).reshape(2, width, wide)
        return carry

    lax.fori_loop(0, chunks, finish_y, 0)

    for s in (0, 1):

        @pl.when(has_r[s])
        def _():
            wy_copy(s, True).wait_recv()

    first, second = (
        jnp.broadcast_to(halves[s] + wy_in[s], (128, 128)).T for s in (0, 1)
    )
    sum_k = jnp.concatenate([first[width:], second[:width]], axis=0)[:, 0:1]
    back_k = scale_k * scale_k * sum_k / features
    for c in range(chunks):
        k_float = k_ref[0, :, :, lanes(c)].reshape(tokens, wide).astype(F32)
        grad_k = own[c, 0, 1:3].reshape(tokens, wide) - k_float * back_k
        ok_ref[0, :, :, lanes(c)] = grad_k.astype(BF16).reshape(2, width, wide)

    for s in (0, 1):

        @pl.when(has_f[s])
        def _():
            wx_copy(s, False).wait_send()

        @pl.when(has_r[s])
        def _():
            wy_copy(s, False).wait_send()

    def drain(c, carry):
        for s in (0, 1):

            @pl.when(has_r[s])
            def _():
                for a in (0, 1):
                    row_out(c, a, s).wait_send()
                gy_copy(c, s, False).wait_send()

            @pl.when(has_f[s])
            def _():
                for a in (0, 1):
                    frame_out(c, a, s).wait_send()
                gx_copy(c, s, False).wait_send()

            for t in (0, 1):

                @pl.when(jnp.logical_and(has_r[t], has_f[s]))
                def _():
                    for a in (0, 1):
                        corner_out(c, a, s, t).wait_send()

        return carry

    lax.fori_loop(0, chunks, drain, 0)


def per_device(sizes, per, q_pre, k_pre, values, target, gain_q, gain_k, kept):
    _, _, width, feat_dev = q_pre.shape
    chunks, wide = feat_dev // (per * HD), per * HD
    dma = pltpu.SemaphoreType.DMA
    vmem = pl.BlockSpec(memory_space=pltpu.VMEM)
    out = jax.ShapeDtypeStruct(q_pre.shape, BF16)
    return pl.pallas_call(
        functools.partial(kernel, sizes, feat_dev * sizes[2]),
        out_shape=(out, out, out),
        in_specs=[pl.BlockSpec(memory_space=pltpu.HBM)] * 7,
        out_specs=(vmem, vmem, vmem),
        scratch_shapes=[
            pltpu.VMEM((chunks, 2, 3, 4, width, wide), BF16),
            pltpu.VMEM((chunks, 2 * width, wide), BF16),
            pltpu.VMEM((2 * width, 12 * width), F32),
            pltpu.VMEM((chunks, 2, 2, 4, width, wide), BF16),
            pltpu.VMEM((chunks, 2, 2, 4, width, wide), BF16),
            pltpu.VMEM((chunks, 2, 2, width, wide), BF16),
            pltpu.VMEM((chunks, 2, 2, width, wide), BF16),
            pltpu.VMEM((chunks, 2, 4, width, wide), F32),
            pltpu.VMEM((chunks, 2 * width, wide), F32),
            pltpu.VMEM((2 * width, HD), F32),
            pltpu.VMEM((2, 8, 128), F32),
            pltpu.VMEM((2, 8, 128), F32),
            dma((chunks, 2, 2)),
            dma((chunks, 2, 2)),
            dma((chunks, 2, 2)),
            dma((chunks, 2, 2)),
            dma((chunks, 2, 2, 2)),
            dma((chunks, 2, 2, 2)),
            dma((chunks, 2)),
            dma((chunks, 2)),
            dma((chunks, 2)),
            dma((chunks, 2)),
            dma((2,)),
            dma((2,)),
            *([pltpu.VMEM(q_pre.shape, BF16)] * 4),
            pltpu.VMEM((1, feat_dev), F32),
            pltpu.VMEM((1, feat_dev), F32),
            pltpu.SMEM((kept.shape[0], TILES, kept.shape[1]), jnp.int32),
            dma((7,)),
            pltpu.VMEM((1, 12 * width), F32),
            pltpu.VMEM((1, 12 * width), F32),
            *([pltpu.VMEM((2, 1, 4 * width), F32)] * 2),
            *([pltpu.VMEM((2, 1, 2 * width), F32)] * 2),
            *([dma((1,))] * 2),
            *([dma((2,))] * 4),
        ],
        compiler_params=pltpu.CompilerParams(vmem_limit_bytes=60 << 20, collective_id=0, has_side_effects=True),
    )(q_pre, k_pre, values, target, gain_q, gain_k, kept.transpose(0, 2, 1))


def solution(mesh):
    sizes = tuple(mesh.shape[a] for a in ("frame", "row", "head"))
    grid = P("frame", "row", None, "head")
    return jax.shard_map(
        functools.partial(per_device, sizes, 2),
        mesh=mesh,
        in_specs=(grid, grid, grid, grid, P("head"), P("head"), P()),
        out_specs=(grid, grid, grid),
        check_vma=False,
    )
```

```python
import functools

import jax
import jax.numpy as jnp
from jax import lax
from jax.experimental import pallas as pl
from jax.experimental.pallas import tpu as pltpu
from jax.sharding import PartitionSpec as P

TC = 16
HD = 128
TILES = 4
MESH = pl.DeviceIdType.MESH
norm_eps = 1e-06
LOG2E = 1.4426950408889634
SCORE_SCALE = HD ** (-0.5)
NEG = -1e30

BF16 = jnp.bfloat16
F32 = jnp.float32
ROWS_T = (((0,), (0,)), ((), ()))
COLS_T = (((1,), (1,)), ((), ()))
PLAIN = (((1,), (0,)), ((), ()))


def dot(a, b, dims):
    return lax.dot_general(a, b, dims, preferred_element_type=F32)


def columns_to_rows(col_a, col_b):
    lane = lax.broadcasted_iota(jnp.int32, (128, 128), 1)
    both = jnp.where(lane < 4, jnp.broadcast_to(col_a, (128, 128)), jnp.broadcast_to(col_b, (128, 128)))
    return both.T[0:8]


def rows_to_columns(rows):
    sub = lax.broadcasted_iota(jnp.int32, (128, 128), 0)
    both = jnp.where(
        sub < 64,
        jnp.broadcast_to(rows[0:1], (128, 128)),
        jnp.broadcast_to(rows[4:5], (128, 128)),
    ).T
    return both[:, 0:1], both[:, 64:65]


def kernel(
    sizes, features, q_hbm, k_hbm, v_hbm, t_hbm, gq_hbm, gk_hbm, kept_hbm,
    oq_ref, ok_ref, ov_ref,
    kv, qn, bias, gx_out, gx_in, gy_out, gy_in, own, dq, acc, hx_out, hx_in,
    row_s, row_r, fr_s, fr_r, co_s, co_r, gx_s, gx_r, gy_s, gy_r, hx_s, hx_r,
    q_ref, k_ref, v_ref, t_ref, gq_ref, gk_ref, kept_ref, load_s,
    w_out, w_in, wx_out, wx_in, wy_out, wy_in, w_s, w_r, wx_s, wx_r, wy_s, wy_r,
):
    frames, rows, heads = sizes
    chunks, _, _, _, width, wide = kv.shape
    per = wide // HD
    tokens = 2 * width
    f_at, r_at, h_at = (lax.axis_index(a) for a in ("frame", "row", "head"))
    frame_id = [(f_at - 1, r_at, h_at), (f_at + 1, r_at, h_at)]
    row_id = [(f_at, r_at - 1, h_at), (f_at, r_at + 1, h_at)]
    head_id = (f_at, r_at, 1 - h_at)
    has_f = [f_at > 0, f_at < frames - 1]
    has_r = [r_at > 0, r_at < rows - 1]

    loads = [
        pltpu.make_async_copy(src, dst, load_s.at[i])
        for i, (src, dst) in enumerate(
            (
                (q_hbm, q_ref), (k_hbm, k_ref), (v_hbm, v_ref), (kept_hbm, kept_ref),
                (gk_hbm, gk_ref.at[0]), (gq_hbm, gq_ref.at[0]), (t_hbm, t_ref),
            )
        )
    ]
    for load in loads:
        load.start()
    barrier = pltpu.get_barrier_semaphore()
    pl.semaphore_signal(barrier, inc=1, device_id=head_id, device_id_type=MESH)
    for s in (0, 1):
        for has, ids in ((has_f, frame_id), (has_r, row_id)):

            @pl.when(has[s])
            def _():
                pl.semaphore_signal(barrier, inc=1, device_id=ids[s], device_id_type=MESH)

    def remote(src, dst, send, recv, device):
        return pltpu.make_async_remote_copy(
            src_ref=src, dst_ref=dst, send_sem=send, recv_sem=recv,
            device_id=device, device_id_type=MESH,
        )

    def row_out(c, a, s):
        return remote(kv.at[c, a, 1, 1 + s], kv.at[c, a, 1, 3 - 3 * s],
                      row_s.at[c, a, s], row_r.at[c, a, 1 - s], row_id[s])

    def row_in(c, a, s):
        return remote(kv.at[c, a, 1, 1 + s], kv.at[c, a, 1, 3 * s],
                      row_s.at[c, a, s], row_r.at[c, a, s], row_id[s])

    def frame_out(c, a, s):
        return remote(kv.at[c, a, 1, pl.ds(1, 2)], kv.at[c, a, 2 - 2 * s, pl.ds(1, 2)],
                      fr_s.at[c, a, s], fr_r.at[c, a, 1 - s], frame_id[s])

    def frame_in(c, a, s):
        return remote(kv.at[c, a, 1, pl.ds(1, 2)], kv.at[c, a, 2 * s, pl.ds(1, 2)],
                      fr_s.at[c, a, s], fr_r.at[c, a, s], frame_id[s])

    def corner_out(c, a, s, t):
        return remote(kv.at[c, a, 1, 3 * t], kv.at[c, a, 2 - 2 * s, 3 * t],
                      co_s.at[c, a, s, t], co_r.at[c, a, 1 - s, t], frame_id[s])

    def corner_in(c, a, s, t):
        return remote(kv.at[c, a, 1, 3 * t], kv.at[c, a, 2 * s, 3 * t],
                      co_s.at[c, a, s, t], co_r.at[c, a, s, t], frame_id[s])

    def corner_row_out(c, a, s, t):
        return remote(kv.at[c, a, 2 * s, 1 + t], kv.at[c, a, 2 * s, 3 - 3 * t],
                      co_s.at[c, a, s, t], co_r.at[c, a, s, 1 - t], row_id[t])

    def gx_copy(c, s, mine):
        return remote(gx_out.at[c, s], gx_in.at[c, s if mine else 1 - s],
                      gx_s.at[c, s], gx_r.at[c, s if mine else 1 - s], frame_id[s])

    def gy_copy(c, s, mine):
        return remote(gy_out.at[c, s], gy_in.at[c, s if mine else 1 - s],
                      gy_s.at[c, s], gy_r.at[c, s if mine else 1 - s], row_id[s])

    def w_copy():
        return remote(w_out, w_in, w_s.at[0], w_r.at[0], head_id)

    def wx_copy(s, mine):
        return remote(wx_out.at[s], wx_in.at[s if mine else 1 - s],
                      wx_s.at[s], wx_r.at[s if mine else 1 - s], frame_id[s])

    def wy_copy(s, mine):
        return remote(wy_out.at[s], wy_in.at[s if mine else 1 - s],
                      wy_s.at[s], wy_r.at[s if mine else 1 - s], row_id[s])

    def hx_copy(i):
        return remote(hx_out.at[i], hx_in.at[i], hx_s.at[i], hx_r.at[i], head_id)

    def lanes(c):
        return slice(c * wide, (c + 1) * wide)

    for s in (0, 1):

        @pl.when(jnp.logical_not(has_f[s]))
        def _():
            wx_in[s] = jnp.zeros((1, 4 * width), F32)

            def body(c, carry):
                kv[c, :, 2 * s] = jnp.zeros((2, 4, width, wide), BF16)
                gx_in[c, s] = jnp.zeros((2, 4, width, wide), BF16)
                return carry

            lax.fori_loop(0, chunks, body, 0)

        @pl.when(jnp.logical_not(has_r[s]))
        def _():
            wy_in[s] = jnp.zeros((1, 2 * width), F32)

            def body(c, carry):
                for a in (0, 1):
                    for d in range(3):
                        kv[c, a, d, 3 * s] = jnp.zeros((width, wide), BF16)
                gy_in[c, s] = jnp.zeros((2, width, wide), BF16)
                return carry

            lax.fori_loop(0, chunks, body, 0)

    loads[0].wait()
    loads[1].wait()
    square_q = jnp.zeros((tokens, 128), F32)
    square_k = jnp.zeros((tokens, 128), F32)
    for i in range(chunks * per):
        part = slice(i * HD, (i + 1) * HD)
        q_part = q_ref[0, :, :, part].reshape(tokens, HD).astype(F32)
        k_part = k_ref[0, :, :, part].reshape(tokens, HD).astype(F32)
        square_q += q_part * q_part
        square_k += k_part * k_part
    hx_out[0] = columns_to_rows(
        jnp.sum(square_q, -1, keepdims=True), jnp.sum(square_k, -1, keepdims=True)
    )

    loads[2].wait()
    for c in range(chunks):
        kv[c, 1, 1, 1:3] = v_ref[0, :, :, lanes(c)]
    peers = 1
    for edge in (*has_f, *has_r):
        peers = peers + edge.astype(jnp.int32)
    pl.semaphore_wait(barrier, peers)

    hx_copy(0).start()

    def send_own(c, a):
        for s in (0, 1):

            @pl.when(has_r[s])
            def _():
                row_out(c, a, s).start()

            @pl.when(has_f[s])
            def _():
                frame_out(c, a, s).start()

    def v_body(c, carry):
        send_own(c, 1)
        return carry

    lax.fori_loop(0, chunks, v_body, 0)

    def relay(a, c, carry):
        @pl.when(c % 2 == 0)
        def _():
            for t in (0, 1):

                @pl.when(has_r[t])
                def _():
                    row_in(c, a, t).wait_recv()

                for s in (0, 1):

                    @pl.when(jnp.logical_and(has_r[t], has_f[s]))
                    def _():
                        corner_out(c, a, s, t).start()

        @pl.when(c % 2 == 1)
        def _():
            for s in (0, 1):

                @pl.when(has_f[s])
                def _():
                    frame_in(c, a, s).wait_recv()

                for t in (0, 1):

                    @pl.when(jnp.logical_and(has_r[t], has_f[s]))
                    def _():
                        corner_row_out(c, a, s, t).start()

        return carry

    loads[3].wait()
    keys = 12 * width
    key = lax.broadcasted_iota(jnp.int32, (1, keys), 1)
    key_line = key // TC
    kept_row = jnp.zeros((1, keys), jnp.int32)
    for d in range(3):
        frame = f_at + (d - 1)
        frame_ok = jnp.logical_and(frame >= 0, frame < frames)
        for g in range(4):
            row = 2 * r_at + (g - 1)
            ok = jnp.logical_and(frame_ok, jnp.logical_and(row >= 0, row < 2 * rows))
            for tile in range(TILES):
                one = kept_ref[jnp.clip(frame, 0, frames - 1), tile, jnp.clip(row, 0, 2 * rows - 1)]
                one = jnp.where(ok, one, 0)
                kept_row = jnp.where(key_line == (d * 4 + g) * TILES + tile, one, kept_row)
    query = lax.broadcasted_iota(jnp.int32, (tokens, keys), 0)
    keyb = lax.broadcasted_iota(jnp.int32, (tokens, keys), 1)
    q_row, q_tile = query // width + 1, (query % width) // TC
    k_line, k_tile = keyb // width, (keyb % width) // TC
    k_row = k_line % 4
    near = (jnp.abs(q_row - k_row) <= 1) & (jnp.abs(q_tile - k_tile) <= 1)
    same = (k_line == q_row + 4) & (q_tile == k_tile)
    kept_full = jnp.broadcast_to(kept_row, (tokens, keys)) > 0
    bias[...] = jnp.where(near & (kept_full | same), 0.0, NEG)

    lax.fori_loop(0, chunks, functools.partial(relay, 1), 0)
    for load in loads[4:]:
        load.wait()
    hx_copy(0).wait()
    scale_q, scale_k = rows_to_columns(
        lax.rsqrt((hx_out[0] + hx_in[0]) / features + norm_eps)
    )
    for c in range(chunks):
        k_norm = k_ref[0, :, :, lanes(c)].reshape(tokens, wide).astype(F32) * scale_k
        k_norm = (k_norm * gk_ref[:, lanes(c)]).astype(BF16)
        kv[c, 0, 1, 1:3] = k_norm.reshape(2, width, wide)
        send_own(c, 0)
    for c in range(chunks):
        q_norm = q_ref[0, :, :, lanes(c)].reshape(tokens, wide).astype(F32) * scale_q
        qn[c] = (q_norm * gq_ref[:, lanes(c)]).astype(BF16)

    lax.fori_loop(0, chunks, functools.partial(relay, 0), 0)

    acc[...] = jnp.zeros_like(acc)
    w_out[...] = jnp.zeros_like(w_out)

    def finish_x(c):
        for s in (0, 1):

            @pl.when(has_f[s])
            def _():
                gx_copy(c, s, True).wait_recv()

        for a in (0, 1):
            for g in range(4):
                total = own[c, a, g] + gx_in[c, 0, a, g].astype(F32) + gx_in[c, 1, a, g].astype(F32)
                if g in (0, 3):
                    gy_out[c, g // 3, a] = total.astype(BF16)
                else:
                    own[c, a, g] = total
        for s in (0, 1):

            @pl.when(has_r[s])
            def _():
                gy_copy(c, s, False).start()

    def compute(c, carry):
        for s in (0, 1):

            @pl.when(jnp.logical_and(has_f[s], c % 2 == 0))
            def _():
                for a in (0, 1):
                    frame_in(c, a, s).wait_recv()

            @pl.when(jnp.logical_and(has_r[s], c % 2 == 1))
            def _():
                for a in (0, 1):
                    row_in(c, a, s).wait_recv()

            for t in (0, 1):

                @pl.when(jnp.logical_and(has_r[t], has_f[s]))
                def _():
                    for a in (0, 1):
                        corner_in(c, a, s, t).wait_recv()

        for j in range(per):
            part = slice(j * HD, (j + 1) * HD)
            at = pl.ds(pl.multiple_of(c * wide + j * HD, HD), HD)
            query_h = qn[c, :, part]
            key_h = kv[c, 0, :, :, :, part].reshape(keys, HD)
            value_h = kv[c, 1, :, :, :, part].reshape(keys, HD)
            inner = dot(query_h, key_h, COLS_T)
            scores = inner * (SCORE_SCALE * LOG2E) + bias[...]
            expo = jnp.exp2(scores - jnp.max(scores, -1, keepdims=True))
            prob = expo * (1.0 / jnp.sum(expo, -1, keepdims=True))
            prob_b = prob.astype(BF16)
            attended = dot(prob_b, value_h, PLAIN)
            target = t_ref[0, :, :, at].reshape(tokens, HD).astype(F32)
            d_out = (attended - target).astype(BF16)
            delta = jnp.sum(d_out.astype(F32) * attended, -1, keepdims=True)
            prob_grad = dot(d_out, value_h, COLS_T)
            score_grad = (prob * ((prob_grad - delta) * SCORE_SCALE)).astype(BF16)
            w_out[...] += jnp.sum(score_grad.astype(F32) * inner, 0, keepdims=True)
            dq_h = dot(score_grad, key_h, PLAIN)
            gated = dq_h * gq_ref[:, at]
            dq[c, :, part] = gated
            acc[...] += gated * q_ref[0, :, :, at].reshape(tokens, HD).astype(F32)
            for a, grad in (
                (0, dot(score_grad, query_h, ROWS_T)),
                (1, dot(prob_b, d_out, ROWS_T)),
            ):
                grad = grad.reshape(3, 4, width, HD)
                own[c, a, :, :, part] = grad[1]
                for s in (0, 1):
                    gx_out[c, s, a, :, :, part] = grad[2 * s].astype(BF16)
        for s in (0, 1):

            @pl.when(has_f[s])
            def _():
                gx_copy(c, s, False).start()

        @pl.when(c >= 2)
        def _():
            finish_x(c - 2)

        return carry

    lax.fori_loop(0, chunks, compute, 0)

    sum_q = jnp.sum(acc[...], -1, keepdims=True)
    hx_out[1] = columns_to_rows(sum_q, sum_q)
    w_copy().start()
    hx_copy(1).start()
    w_copy().wait()
    both = w_out[...] + w_in[...]
    for s in (0, 1):
        wx_out[s] = both[:, 8 * s * width : (8 * s + 4) * width]

        @pl.when(has_f[s])
        def _():
            wx_copy(s, False).start()

    hx_copy(1).wait()
    sum_q, _ = rows_to_columns((hx_out[1] + hx_in[1]) / features)
    back_q = scale_q * scale_q * scale_q * sum_q
    for c in range(chunks):
        q_float = q_ref[0, :, :, lanes(c)].reshape(tokens, wide).astype(F32)
        grad_q = scale_q * dq[c] - q_float * back_q
        oq_ref[0, :, :, lanes(c)] = grad_q.astype(BF16).reshape(2, width, wide)

    def last_x(c, carry):
        finish_x(c)
        return carry

    lax.fori_loop(max(chunks - 2, 0), chunks, last_x, 0)

    for s in (0, 1):

        @pl.when(has_f[s])
        def _():
            wx_copy(s, True).wait_recv()

    mine = both[:, 4 * width : 8 * width] + wx_in[0] + wx_in[1]
    halves = [mine[:, 0 : 2 * width], mine[:, 2 * width : 4 * width]]
    for s in (0, 1):
        wy_out[s] = halves[s]

        @pl.when(has_r[s])
        def _():
            wy_copy(s, False).start()

    def finish_y(c, carry):
        at = pl.ds(pl.multiple_of(c * wide, HD), wide)
        for s in (0, 1):

            @pl.when(has_r[s])
            def _():
                gy_copy(c, s, True).wait_recv()

        ov_ref[0, :, :, at] = (own[c, 1, 1:3] + gy_in[c, :, 1].astype(F32)).astype(BF16)
        gated = (own[c, 0, 1:3] + gy_in[c, :, 0].astype(F32)).reshape(tokens, wide) * gk_ref[:, at]
        own[c, 0, 1:3] = (gated * scale_k).reshape(2, width, wide)
        return carry

    lax.fori_loop(0, chunks, finish_y, 0)

    for s in (0, 1):

        @pl.when(has_r[s])
        def _():
            wy_copy(s, True).wait_recv()

    first, second = (
        jnp.broadcast_to(halves[s] + wy_in[s], (128, 128)).T for s in (0, 1)
    )
    sum_k = jnp.concatenate([first[width:], second[:width]], axis=0)[:, 0:1]
    back_k = scale_k * scale_k * sum_k / features
    for c in range(chunks):
        k_float = k_ref[0, :, :, lanes(c)].reshape(tokens, wide).astype(F32)
        grad_k = own[c, 0, 1:3].reshape(tokens, wide) - k_float * back_k
        ok_ref[0, :, :, lanes(c)] = grad_k.astype(BF16).reshape(2, width, wide)

    for s in (0, 1):

        @pl.when(has_f[s])
        def _():
            wx_copy(s, False).wait_send()

        @pl.when(has_r[s])
        def _():
            wy_copy(s, False).wait_send()

    def drain(c, carry):
        for s in (0, 1):

            @pl.when(has_r[s])
            def _():
                for a in (0, 1):
                    row_out(c, a, s).wait_send()
                gy_copy(c, s, False).wait_send()

            @pl.when(has_f[s])
            def _():
                for a in (0, 1):
                    frame_out(c, a, s).wait_send()
                gx_copy(c, s, False).wait_send()

            for t in (0, 1):

                @pl.when(jnp.logical_and(has_r[t], has_f[s]))
                def _():
                    for a in (0, 1):
                        corner_out(c, a, s, t).wait_send()

        return carry

    lax.fori_loop(0, chunks, drain, 0)


def hand_over(*refs):
    sources, results, (held, in_s, out_s) = refs[:3], refs[3:6], refs[6:]
    moves = [
        (
            pltpu.make_async_copy(sources[i], held.at[i], in_s.at[i]),
            pltpu.make_async_copy(held.at[i], results[i], out_s.at[i]),
        )
        for i in range(3)
    ]
    for take, _ in moves:
        take.start()
    for take, give in moves:
        take.wait()
        give.start()
    for _, give in moves:
        give.wait()


def per_device(sizes, per, q_pre, k_pre, values, target, gain_q, gain_k, kept):
    _, _, width, feat_dev = q_pre.shape
    chunks, wide = feat_dev // (per * HD), per * HD
    dma = pltpu.SemaphoreType.DMA
    vmem = pl.BlockSpec(memory_space=pltpu.VMEM)
    out = jax.ShapeDtypeStruct(q_pre.shape, BF16)
    grads = pl.pallas_call(
        functools.partial(kernel, sizes, feat_dev * sizes[2]),
        out_shape=(out, out, out),
        in_specs=[pl.BlockSpec(memory_space=pltpu.HBM)] * 7,
        out_specs=(vmem, vmem, vmem),
        scratch_shapes=[
            pltpu.VMEM((chunks, 2, 3, 4, width, wide), BF16),
            pltpu.VMEM((chunks, 2 * width, wide), BF16),
            pltpu.VMEM((2 * width, 12 * width), F32),
            pltpu.VMEM((chunks, 2, 2, 4, width, wide), BF16),
            pltpu.VMEM((chunks, 2, 2, 4, width, wide), BF16),
            pltpu.VMEM((chunks, 2, 2, width, wide), BF16),
            pltpu.VMEM((chunks, 2, 2, width, wide), BF16),
            pltpu.VMEM((chunks, 2, 4, width, wide), F32),
            pltpu.VMEM((chunks, 2 * width, wide), F32),
            pltpu.VMEM((2 * width, HD), F32),
            pltpu.VMEM((2, 8, 128), F32),
            pltpu.VMEM((2, 8, 128), F32),
            dma((chunks, 2, 2)),
            dma((chunks, 2, 2)),
            dma((chunks, 2, 2)),
            dma((chunks, 2, 2)),
            dma((chunks, 2, 2, 2)),
            dma((chunks, 2, 2, 2)),
            dma((chunks, 2)),
            dma((chunks, 2)),
            dma((chunks, 2)),
            dma((chunks, 2)),
            dma((2,)),
            dma((2,)),
            *([pltpu.VMEM(q_pre.shape, BF16)] * 4),
            pltpu.VMEM((1, feat_dev), F32),
            pltpu.VMEM((1, feat_dev), F32),
            pltpu.SMEM((kept.shape[0], TILES, kept.shape[1]), jnp.int32),
            dma((7,)),
            pltpu.VMEM((1, 12 * width), F32),
            pltpu.VMEM((1, 12 * width), F32),
            *([pltpu.VMEM((2, 1, 4 * width), F32)] * 2),
            *([pltpu.VMEM((2, 1, 2 * width), F32)] * 2),
            *([dma((1,))] * 2),
            *([dma((2,))] * 4),
        ],
        compiler_params=pltpu.CompilerParams(vmem_limit_bytes=60 << 20, collective_id=0, has_side_effects=True),
    )(q_pre, k_pre, values, target, gain_q, gain_k, kept.transpose(0, 2, 1))
    hbm = pl.BlockSpec(memory_space=pltpu.HBM)
    return pl.pallas_call(
        hand_over,
        out_shape=(out, out, out),
        in_specs=[hbm] * 3,
        out_specs=(hbm, hbm, hbm),
        scratch_shapes=[pltpu.VMEM((3, *q_pre.shape), BF16), dma((3,)), dma((3,))],
        compiler_params=pltpu.CompilerParams(vmem_limit_bytes=60 << 20),
    )(*grads)


def solution(mesh):
    sizes = tuple(mesh.shape[a] for a in ("frame", "row", "head"))
    grid = P("frame", "row", None, "head")
    return jax.shard_map(
        functools.partial(per_device, sizes, 2),
        mesh=mesh,
        in_specs=(grid, grid, grid, grid, P("head"), P("head"), P()),
        out_specs=(grid, grid, grid),
        check_vma=False,
    )
```

```python
import functools

import jax
import jax.numpy as jnp
from jax import lax
from jax.experimental import pallas as pl
from jax.experimental.pallas import tpu as pltpu
from jax.sharding import PartitionSpec as P

TC = 16
HD = 128
TILES = 4
MESH = pl.DeviceIdType.MESH
norm_eps = 1e-06
LOG2E = 1.4426950408889634
SCORE_SCALE = HD ** (-0.5)
NEG = -1e30

BF16 = jnp.bfloat16
F32 = jnp.float32
ROWS_T = (((0,), (0,)), ((), ()))
COLS_T = (((1,), (1,)), ((), ()))
PLAIN = (((1,), (0,)), ((), ()))


def dot(a, b, dims):
    return lax.dot_general(a, b, dims, preferred_element_type=F32)


def columns_to_rows(col_a, col_b):
    lane = lax.broadcasted_iota(jnp.int32, (128, 128), 1)
    both = jnp.where(lane < 4, jnp.broadcast_to(col_a, (128, 128)), jnp.broadcast_to(col_b, (128, 128)))
    return both.T[0:8]


def rows_to_columns(rows):
    sub = lax.broadcasted_iota(jnp.int32, (128, 128), 0)
    both = jnp.where(
        sub < 64,
        jnp.broadcast_to(rows[0:1], (128, 128)),
        jnp.broadcast_to(rows[4:5], (128, 128)),
    ).T
    return both[:, 0:1], both[:, 64:65]


def kernel(
    sizes, features, q_hbm, k_hbm, v_hbm, t_hbm, gq_hbm, gk_hbm, kept_hbm,
    oq_ref, ok_ref, ov_ref,
    kv, qn, bias, gx_out, gx_in, gy_out, gy_in, own, dq, acc, hx_out, hx_in,
    row_s, row_r, fr_s, fr_r, co_s, co_r, gx_s, gx_r, gy_s, gy_r, hx_s, hx_r,
    q_ref, k_ref, v_ref, t_ref, gq_ref, gk_ref, kept_ref, load_s,
    w_out, w_in, wx_out, wx_in, wy_out, wy_in, w_s, w_r, wx_s, wx_r, wy_s, wy_r,
    gc_in, gc_s, gc_r,
):
    frames, rows, heads = sizes
    chunks, _, _, _, width, wide = kv.shape
    per = wide // HD
    tokens = 2 * width
    f_at, r_at, h_at = (lax.axis_index(a) for a in ("frame", "row", "head"))
    frame_id = [(f_at - 1, r_at, h_at), (f_at + 1, r_at, h_at)]
    row_id = [(f_at, r_at - 1, h_at), (f_at, r_at + 1, h_at)]
    head_id = (f_at, r_at, 1 - h_at)
    has_f = [f_at > 0, f_at < frames - 1]
    has_r = [r_at > 0, r_at < rows - 1]

    loads = [
        pltpu.make_async_copy(src, dst, load_s.at[i])
        for i, (src, dst) in enumerate(
            (
                (q_hbm, q_ref), (k_hbm, k_ref), (v_hbm, v_ref), (kept_hbm, kept_ref),
                (gk_hbm, gk_ref.at[0]), (gq_hbm, gq_ref.at[0]), (t_hbm, t_ref),
            )
        )
    ]
    for load in loads:
        load.start()
    barrier = pltpu.get_barrier_semaphore()
    pl.semaphore_signal(barrier, inc=1, device_id=head_id, device_id_type=MESH)
    for s in (0, 1):
        for has, ids in ((has_f, frame_id), (has_r, row_id)):

            @pl.when(has[s])
            def _():
                pl.semaphore_signal(barrier, inc=1, device_id=ids[s], device_id_type=MESH)

    def remote(src, dst, send, recv, device):
        return pltpu.make_async_remote_copy(
            src_ref=src, dst_ref=dst, send_sem=send, recv_sem=recv,
            device_id=device, device_id_type=MESH,
        )

    def row_out(c, a, s):
        return remote(kv.at[c, a, 1, 1 + s], kv.at[c, a, 1, 3 - 3 * s],
                      row_s.at[c, a, s], row_r.at[c, a, 1 - s], row_id[s])

    def row_in(c, a, s):
        return remote(kv.at[c, a, 1, 1 + s], kv.at[c, a, 1, 3 * s],
                      row_s.at[c, a, s], row_r.at[c, a, s], row_id[s])

    def frame_out(c, a, s):
        return remote(kv.at[c, a, 1, pl.ds(1, 2)], kv.at[c, a, 2 - 2 * s, pl.ds(1, 2)],
                      fr_s.at[c, a, s], fr_r.at[c, a, 1 - s], frame_id[s])

    def frame_in(c, a, s):
        return remote(kv.at[c, a, 1, pl.ds(1, 2)], kv.at[c, a, 2 * s, pl.ds(1, 2)],
                      fr_s.at[c, a, s], fr_r.at[c, a, s], frame_id[s])

    def corner_out(c, a, s, t):
        return remote(kv.at[c, a, 1, 3 * t], kv.at[c, a, 2 - 2 * s, 3 * t],
                      co_s.at[c, a, s, t], co_r.at[c, a, 1 - s, t], frame_id[s])

    def corner_in(c, a, s, t):
        return remote(kv.at[c, a, 1, 3 * t], kv.at[c, a, 2 * s, 3 * t],
                      co_s.at[c, a, s, t], co_r.at[c, a, s, t], frame_id[s])

    def corner_row_out(c, a, s, t):
        return remote(kv.at[c, a, 2 * s, 1 + t], kv.at[c, a, 2 * s, 3 - 3 * t],
                      co_s.at[c, a, s, t], co_r.at[c, a, s, 1 - t], row_id[t])

    def gx_copy(c, s, mine):
        return remote(gx_out.at[c, s], gx_in.at[c, s if mine else 1 - s],
                      gx_s.at[c, s], gx_r.at[c, s if mine else 1 - s], frame_id[s])

    def gx_half(c, s, mine):
        return remote(gx_out.at[c, s, :, pl.ds(1, 2)], gx_in.at[c, s if mine else 1 - s, :, pl.ds(1, 2)],
                      gx_s.at[c, s], gx_r.at[c, s if mine else 1 - s], frame_id[s])

    def gc_copy(c, t, s, mine):
        return remote(gx_out.at[c, s, :, 3 * t], gc_in.at[c, t if mine else 1 - t, s],
                      gc_s.at[c, t, s], gc_r.at[c, t if mine else 1 - t, s], row_id[t])

    def gy_copy(c, s, mine):
        return remote(gy_out.at[c, s], gy_in.at[c, s if mine else 1 - s],
                      gy_s.at[c, s], gy_r.at[c, s if mine else 1 - s], row_id[s])

    def w_copy():
        return remote(w_out, w_in, w_s.at[0], w_r.at[0], head_id)

    def wx_copy(s, mine):
        return remote(wx_out.at[s], wx_in.at[s if mine else 1 - s],
                      wx_s.at[s], wx_r.at[s if mine else 1 - s], frame_id[s])

    def wy_copy(s, mine):
        return remote(wy_out.at[s], wy_in.at[s if mine else 1 - s],
                      wy_s.at[s], wy_r.at[s if mine else 1 - s], row_id[s])

    def hx_copy(i):
        return remote(hx_out.at[i], hx_in.at[i], hx_s.at[i], hx_r.at[i], head_id)

    def lanes(c):
        return slice(c * wide, (c + 1) * wide)

    for s in (0, 1):

        @pl.when(jnp.logical_not(has_f[s]))
        def _():
            wx_in[s] = jnp.zeros((1, 4 * width), F32)

            def body(c, carry):
                kv[c, :, 2 * s] = jnp.zeros((2, 4, width, wide), BF16)
                gx_in[c, s] = jnp.zeros((2, 4, width, wide), BF16)
                return carry

            lax.fori_loop(0, chunks, body, 0)

        @pl.when(jnp.logical_not(has_r[s]))
        def _():
            wy_in[s] = jnp.zeros((1, 2 * width), F32)

            def body(c, carry):
                for a in (0, 1):
                    for d in range(3):
                        kv[c, a, d, 3 * s] = jnp.zeros((width, wide), BF16)
                gy_in[c, s] = jnp.zeros((2, width, wide), BF16)
                gc_in[c, s] = jnp.zeros((2, 2, width, wide), BF16)
                return carry

            lax.fori_loop(0, chunks, body, 0)

    loads[0].wait()
    loads[1].wait()
    square_q = jnp.zeros((tokens, 128), F32)
    square_k = jnp.zeros((tokens, 128), F32)
    for i in range(chunks * per):
        part = slice(i * HD, (i + 1) * HD)
        q_part = q_ref[0, :, :, part].reshape(tokens, HD).astype(F32)
        k_part = k_ref[0, :, :, part].reshape(tokens, HD).astype(F32)
        square_q += q_part * q_part
        square_k += k_part * k_part
    hx_out[0] = columns_to_rows(
        jnp.sum(square_q, -1, keepdims=True), jnp.sum(square_k, -1, keepdims=True)
    )

    loads[2].wait()
    for c in range(chunks):
        kv[c, 1, 1, 1:3] = v_ref[0, :, :, lanes(c)]
    peers = 1
    for edge in (*has_f, *has_r):
        peers = peers + edge.astype(jnp.int32)
    pl.semaphore_wait(barrier, peers)

    hx_copy(0).start()

    def send_own(c, a):
        for s in (0, 1):

            @pl.when(has_r[s])
            def _():
                row_out(c, a, s).start()

            @pl.when(has_f[s])
            def _():
                frame_out(c, a, s).start()

    def v_body(c, carry):
        send_own(c, 1)
        return carry

    lax.fori_loop(0, chunks, v_body, 0)

    def relay(a, c, carry):
        @pl.when(c % 2 == 0)
        def _():
            for t in (0, 1):

                @pl.when(has_r[t])
                def _():
                    row_in(c, a, t).wait_recv()

                for s in (0, 1):

                    @pl.when(jnp.logical_and(has_r[t], has_f[s]))
                    def _():
                        corner_out(c, a, s, t).start()

        @pl.when(c % 2 == 1)
        def _():
            for s in (0, 1):

                @pl.when(has_f[s])
                def _():
                    frame_in(c, a, s).wait_recv()

                for t in (0, 1):

                    @pl.when(jnp.logical_and(has_r[t], has_f[s]))
                    def _():
                        corner_row_out(c, a, s, t).start()

        return carry

    loads[3].wait()
    keys = 12 * width
    key = lax.broadcasted_iota(jnp.int32, (1, keys), 1)
    key_line = key // TC
    kept_row = jnp.zeros((1, keys), jnp.int32)
    for d in range(3):
        frame = f_at + (d - 1)
        frame_ok = jnp.logical_and(frame >= 0, frame < frames)
        for g in range(4):
            row = 2 * r_at + (g - 1)
            ok = jnp.logical_and(frame_ok, jnp.logical_and(row >= 0, row < 2 * rows))
            for tile in range(TILES):
                one = kept_ref[jnp.clip(frame, 0, frames - 1), tile, jnp.clip(row, 0, 2 * rows - 1)]
                one = jnp.where(ok, one, 0)
                kept_row = jnp.where(key_line == (d * 4 + g) * TILES + tile, one, kept_row)
    query = lax.broadcasted_iota(jnp.int32, (tokens, keys), 0)
    keyb = lax.broadcasted_iota(jnp.int32, (tokens, keys), 1)
    q_row, q_tile = query // width + 1, (query % width) // TC
    k_line, k_tile = keyb // width, (keyb % width) // TC
    k_row = k_line % 4
    near = (jnp.abs(q_row - k_row) <= 1) & (jnp.abs(q_tile - k_tile) <= 1)
    same = (k_line == q_row + 4) & (q_tile == k_tile)
    kept_full = jnp.broadcast_to(kept_row, (tokens, keys)) > 0
    bias[...] = jnp.where(near & (kept_full | same), 0.0, NEG)

    lax.fori_loop(0, chunks, functools.partial(relay, 1), 0)
    for load in loads[4:]:
        load.wait()
    hx_copy(0).wait()
    scale_q, scale_k = rows_to_columns(
        lax.rsqrt((hx_out[0] + hx_in[0]) / features + norm_eps)
    )
    for c in range(chunks):
        k_norm = k_ref[0, :, :, lanes(c)].reshape(tokens, wide).astype(F32) * scale_k
        k_norm = (k_norm * gk_ref[:, lanes(c)]).astype(BF16)
        kv[c, 0, 1, 1:3] = k_norm.reshape(2, width, wide)
        send_own(c, 0)
    for c in range(chunks):
        q_norm = q_ref[0, :, :, lanes(c)].reshape(tokens, wide).astype(F32) * scale_q
        qn[c] = (q_norm * gq_ref[:, lanes(c)]).astype(BF16)

    lax.fori_loop(0, chunks, functools.partial(relay, 0), 0)

    acc[...] = jnp.zeros_like(acc)
    w_out[...] = jnp.zeros_like(w_out)

    def finish_x(c):
        for s in (0, 1):

            @pl.when(has_f[s])
            def _():
                gx_copy(c, s, True).wait_recv()

        for a in (0, 1):
            for g in range(4):
                total = own[c, a, g] + gx_in[c, 0, a, g].astype(F32) + gx_in[c, 1, a, g].astype(F32)
                if g in (0, 3):
                    gy_out[c, g // 3, a] = total.astype(BF16)
                else:
                    own[c, a, g] = total
        for s in (0, 1):

            @pl.when(has_r[s])
            def _():
                gy_copy(c, s, False).start()

    def finish_rows(c):
        for t in (0, 1):

            @pl.when(has_r[t])
            def _():
                gy_copy(c, t, True).wait_recv()

            for s in (0, 1):

                @pl.when(jnp.logical_and(has_r[t], has_f[s]))
                def _():
                    gc_copy(c, t, s, True).wait_recv()

        for a in (0, 1):
            for t in (0, 1):
                own[c, a, 1 + t] += gy_in[c, t, a].astype(F32)
                for s in (0, 1):
                    total = gx_out[c, s, a, 1 + t].astype(F32) + gc_in[c, t, s, a].astype(F32)
                    gx_out[c, s, a, 1 + t] = total.astype(BF16)
        for s in (0, 1):

            @pl.when(has_f[s])
            def _():
                gx_half(c, s, False).start()

    def finish_first(c):
        @pl.when(c % 2 == 0)
        def _():
            finish_x(c)

        @pl.when(c % 2 == 1)
        def _():
            finish_rows(c)

    def compute(c, carry):
        for s in (0, 1):

            @pl.when(jnp.logical_and(has_f[s], c % 2 == 0))
            def _():
                for a in (0, 1):
                    frame_in(c, a, s).wait_recv()

            @pl.when(jnp.logical_and(has_r[s], c % 2 == 1))
            def _():
                for a in (0, 1):
                    row_in(c, a, s).wait_recv()

            for t in (0, 1):

                @pl.when(jnp.logical_and(has_r[t], has_f[s]))
                def _():
                    for a in (0, 1):
                        corner_in(c, a, s, t).wait_recv()

        for j in range(per):
            part = slice(j * HD, (j + 1) * HD)
            at = pl.ds(pl.multiple_of(c * wide + j * HD, HD), HD)
            query_h = qn[c, :, part]
            key_h = kv[c, 0, :, :, :, part].reshape(keys, HD)
            value_h = kv[c, 1, :, :, :, part].reshape(keys, HD)
            inner = dot(query_h, key_h, COLS_T)
            scores = inner * (SCORE_SCALE * LOG2E) + bias[...]
            expo = jnp.exp2(scores - jnp.max(scores, -1, keepdims=True))
            prob = expo * (1.0 / jnp.sum(expo, -1, keepdims=True))
            prob_b = prob.astype(BF16)
            attended = dot(prob_b, value_h, PLAIN)
            target = t_ref[0, :, :, at].reshape(tokens, HD).astype(F32)
            d_out = (attended - target).astype(BF16)
            delta = jnp.sum(d_out.astype(F32) * attended, -1, keepdims=True)
            prob_grad = dot(d_out, value_h, COLS_T)
            score_grad = (prob * ((prob_grad - delta) * SCORE_SCALE)).astype(BF16)
            w_out[...] += jnp.sum(score_grad.astype(F32) * inner, 0, keepdims=True)
            dq_h = dot(score_grad, key_h, PLAIN)
            gated = dq_h * gq_ref[:, at]
            dq[c, :, part] = gated
            acc[...] += gated * q_ref[0, :, :, at].reshape(tokens, HD).astype(F32)
            for a, grad in (
                (0, dot(score_grad, query_h, ROWS_T)),
                (1, dot(prob_b, d_out, ROWS_T)),
            ):
                grad = grad.reshape(3, 4, width, HD)
                own[c, a, :, :, part] = grad[1]
                for t in (0, 1):
                    gy_out[c, t, a, :, part] = grad[1, 3 * t].astype(BF16)
                for s in (0, 1):
                    gx_out[c, s, a, :, :, part] = grad[2 * s].astype(BF16)
        for s in (0, 1):

            @pl.when(jnp.logical_and(has_f[s], c % 2 == 0))
            def _():
                gx_copy(c, s, False).start()

            @pl.when(jnp.logical_and(has_r[s], c % 2 == 1))
            def _():
                gy_copy(c, s, False).start()

            for t in (0, 1):

                @pl.when(jnp.logical_and(jnp.logical_and(has_r[t], has_f[s]), c % 2 == 1))
                def _():
                    gc_copy(c, t, s, False).start()

        @pl.when(c >= 2)
        def _():
            finish_first(c - 2)

        return carry

    lax.fori_loop(0, chunks, compute, 0)

    sum_q = jnp.sum(acc[...], -1, keepdims=True)
    hx_out[1] = columns_to_rows(sum_q, sum_q)
    w_copy().start()
    hx_copy(1).start()
    w_copy().wait()
    both = w_out[...] + w_in[...]
    for s in (0, 1):
        wx_out[s] = both[:, 8 * s * width : (8 * s + 4) * width]

        @pl.when(has_f[s])
        def _():
            wx_copy(s, False).start()

    hx_copy(1).wait()
    sum_q, _ = rows_to_columns((hx_out[1] + hx_in[1]) / features)
    back_q = scale_q * scale_q * scale_q * sum_q
    for c in range(chunks):
        q_float = q_ref[0, :, :, lanes(c)].reshape(tokens, wide).astype(F32)
        grad_q = scale_q * dq[c] - q_float * back_q
        oq_ref[0, :, :, lanes(c)] = grad_q.astype(BF16).reshape(2, width, wide)

    def last_x(c, carry):
        finish_first(c)
        return carry

    lax.fori_loop(max(chunks - 2, 0), chunks, last_x, 0)

    for s in (0, 1):

        @pl.when(has_f[s])
        def _():
            wx_copy(s, True).wait_recv()

    mine = both[:, 4 * width : 8 * width] + wx_in[0] + wx_in[1]
    halves = [mine[:, 0 : 2 * width], mine[:, 2 * width : 4 * width]]
    for s in (0, 1):
        wy_out[s] = halves[s]

        @pl.when(has_r[s])
        def _():
            wy_copy(s, False).start()

    def finish_last(c, carry):
        def put(a, total):
            at = pl.ds(pl.multiple_of(c * wide, HD), wide)
            if a == 1:
                ov_ref[0, :, :, at] = total.astype(BF16)
            else:
                gated = total.reshape(tokens, wide) * gk_ref[:, at]
                own[c, 0, 1:3] = (gated * scale_k).reshape(2, width, wide)

        @pl.when(c % 2 == 0)
        def _():
            for s in (0, 1):

                @pl.when(has_r[s])
                def _():
                    gy_copy(c, s, True).wait_recv()

            for a in (0, 1):
                put(a, own[c, a, 1:3] + gy_in[c, :, a].astype(F32))

        @pl.when(c % 2 == 1)
        def _():
            for s in (0, 1):

                @pl.when(has_f[s])
                def _():
                    gx_half(c, s, True).wait_recv()

            for a in (0, 1):
                moved = gx_in[c, 0, a, 1:3].astype(F32) + gx_in[c, 1, a, 1:3].astype(F32)
                put(a, own[c, a, 1:3] + moved)

        return carry

    lax.fori_loop(0, chunks, finish_last, 0)

    for s in (0, 1):

        @pl.when(has_r[s])
        def _():
            wy_copy(s, True).wait_recv()

    first, second = (
        jnp.broadcast_to(halves[s] + wy_in[s], (128, 128)).T for s in (0, 1)
    )
    sum_k = jnp.concatenate([first[width:], second[:width]], axis=0)[:, 0:1]
    back_k = scale_k * scale_k * sum_k / features
    for c in range(chunks):
        k_float = k_ref[0, :, :, lanes(c)].reshape(tokens, wide).astype(F32)
        grad_k = own[c, 0, 1:3].reshape(tokens, wide) - k_float * back_k
        ok_ref[0, :, :, lanes(c)] = grad_k.astype(BF16).reshape(2, width, wide)

    for s in (0, 1):

        @pl.when(has_f[s])
        def _():
            wx_copy(s, False).wait_send()

        @pl.when(has_r[s])
        def _():
            wy_copy(s, False).wait_send()

    def drain(c, carry):
        for s in (0, 1):

            @pl.when(has_r[s])
            def _():
                for a in (0, 1):
                    row_out(c, a, s).wait_send()
                gy_copy(c, s, False).wait_send()

            @pl.when(has_f[s])
            def _():
                for a in (0, 1):
                    frame_out(c, a, s).wait_send()

            @pl.when(jnp.logical_and(has_f[s], c % 2 == 0))
            def _():
                gx_copy(c, s, False).wait_send()

            @pl.when(jnp.logical_and(has_f[s], c % 2 == 1))
            def _():
                gx_half(c, s, False).wait_send()

            for t in (0, 1):

                @pl.when(jnp.logical_and(has_r[t], has_f[s]))
                def _():
                    for a in (0, 1):
                        corner_out(c, a, s, t).wait_send()

                @pl.when(jnp.logical_and(jnp.logical_and(has_r[t], has_f[s]), c % 2 == 1))
                def _():
                    gc_copy(c, t, s, False).wait_send()

        return carry

    lax.fori_loop(0, chunks, drain, 0)


def hand_over(*refs):
    sources, results, (held, in_s, out_s) = refs[:3], refs[3:6], refs[6:]
    moves = [
        (
            pltpu.make_async_copy(sources[i], held.at[i], in_s.at[i]),
            pltpu.make_async_copy(held.at[i], results[i], out_s.at[i]),
        )
        for i in range(3)
    ]
    for take, _ in moves:
        take.start()
    for take, give in moves:
        take.wait()
        give.start()
    for _, give in moves:
        give.wait()


def per_device(sizes, per, q_pre, k_pre, values, target, gain_q, gain_k, kept):
    _, _, width, feat_dev = q_pre.shape
    chunks, wide = feat_dev // (per * HD), per * HD
    dma = pltpu.SemaphoreType.DMA
    vmem = pl.BlockSpec(memory_space=pltpu.VMEM)
    out = jax.ShapeDtypeStruct(q_pre.shape, BF16)
    grads = pl.pallas_call(
        functools.partial(kernel, sizes, feat_dev * sizes[2]),
        out_shape=(out, out, out),
        in_specs=[pl.BlockSpec(memory_space=pltpu.HBM)] * 7,
        out_specs=(vmem, vmem, vmem),
        scratch_shapes=[
            pltpu.VMEM((chunks, 2, 3, 4, width, wide), BF16),
            pltpu.VMEM((chunks, 2 * width, wide), BF16),
            pltpu.VMEM((2 * width, 12 * width), F32),
            pltpu.VMEM((chunks, 2, 2, 4, width, wide), BF16),
            pltpu.VMEM((chunks, 2, 2, 4, width, wide), BF16),
            pltpu.VMEM((chunks, 2, 2, width, wide), BF16),
            pltpu.VMEM((chunks, 2, 2, width, wide), BF16),
            pltpu.VMEM((chunks, 2, 4, width, wide), F32),
            pltpu.VMEM((chunks, 2 * width, wide), F32),
            pltpu.VMEM((2 * width, HD), F32),
            pltpu.VMEM((2, 8, 128), F32),
            pltpu.VMEM((2, 8, 128), F32),
            dma((chunks, 2, 2)),
            dma((chunks, 2, 2)),
            dma((chunks, 2, 2)),
            dma((chunks, 2, 2)),
            dma((chunks, 2, 2, 2)),
            dma((chunks, 2, 2, 2)),
            dma((chunks, 2)),
            dma((chunks, 2)),
            dma((chunks, 2)),
            dma((chunks, 2)),
            dma((2,)),
            dma((2,)),
            *([pltpu.VMEM(q_pre.shape, BF16)] * 4),
            pltpu.VMEM((1, feat_dev), F32),
            pltpu.VMEM((1, feat_dev), F32),
            pltpu.SMEM((kept.shape[0], TILES, kept.shape[1]), jnp.int32),
            dma((7,)),
            pltpu.VMEM((1, 12 * width), F32),
            pltpu.VMEM((1, 12 * width), F32),
            *([pltpu.VMEM((2, 1, 4 * width), F32)] * 2),
            *([pltpu.VMEM((2, 1, 2 * width), F32)] * 2),
            *([dma((1,))] * 2),
            *([dma((2,))] * 4),
            pltpu.VMEM((chunks, 2, 2, 2, width, wide), BF16),
            *([dma((chunks, 2, 2))] * 2),
        ],
        compiler_params=pltpu.CompilerParams(vmem_limit_bytes=60 << 20, collective_id=0, has_side_effects=True),
    )(q_pre, k_pre, values, target, gain_q, gain_k, kept.transpose(0, 2, 1))
    hbm = pl.BlockSpec(memory_space=pltpu.HBM)
    return pl.pallas_call(
        hand_over,
        out_shape=(out, out, out),
        in_specs=[hbm] * 3,
        out_specs=(hbm, hbm, hbm),
        scratch_shapes=[pltpu.VMEM((3, *q_pre.shape), BF16), dma((3,)), dma((3,))],
        compiler_params=pltpu.CompilerParams(vmem_limit_bytes=60 << 20),
    )(*grads)


def solution(mesh):
    sizes = tuple(mesh.shape[a] for a in ("frame", "row", "head"))
    grid = P("frame", "row", None, "head")
    return jax.shard_map(
        functools.partial(per_device, sizes, 2),
        mesh=mesh,
        in_specs=(grid, grid, grid, grid, P("head"), P("head"), P()),
        out_specs=(grid, grid, grid),
        check_vma=False,
    )
```

```python
import functools

import jax
import jax.numpy as jnp
from jax import lax
from jax.experimental import pallas as pl
from jax.experimental.pallas import tpu as pltpu
from jax.sharding import PartitionSpec as P

TC = 16
HD = 128
TILES = 4
MESH = pl.DeviceIdType.MESH
norm_eps = 1e-06
LOG2E = 1.4426950408889634
SCORE_SCALE = HD ** (-0.5)
NEG = -1e30

BF16 = jnp.bfloat16
F32 = jnp.float32
ROWS_T = (((0,), (0,)), ((), ()))
COLS_T = (((1,), (1,)), ((), ()))
PLAIN = (((1,), (0,)), ((), ()))


def dot(a, b, dims):
    return lax.dot_general(a, b, dims, preferred_element_type=F32)


def columns_to_rows(col_a, col_b):
    lane = lax.broadcasted_iota(jnp.int32, (128, 128), 1)
    both = jnp.where(lane < 4, jnp.broadcast_to(col_a, (128, 128)), jnp.broadcast_to(col_b, (128, 128)))
    return both.T[0:8]


def rows_to_columns(rows):
    sub = lax.broadcasted_iota(jnp.int32, (128, 128), 0)
    both = jnp.where(
        sub < 64,
        jnp.broadcast_to(rows[0:1], (128, 128)),
        jnp.broadcast_to(rows[4:5], (128, 128)),
    ).T
    return both[:, 0:1], both[:, 64:65]


def kernel(
    sizes, features, q_hbm, k_hbm, v_hbm, t_hbm, gq_hbm, gk_hbm, kept_hbm,
    oq_ref, ok_ref, ov_ref,
    kv, qn, bias, gx_out, gx_in, gy_out, gy_in, own, dq, acc, hx_out, hx_in,
    row_s, row_r, fr_s, fr_r, co_s, co_r, gx_s, gx_r, gy_s, gy_r, hx_s, hx_r,
    q_ref, k_ref, v_ref, t_ref, gq_ref, gk_ref, kept_ref, load_s,
    w_out, w_in, wx_out, wx_in, wy_out, wy_in, w_s, w_r, wx_s, wx_r, wy_s, wy_r,
):
    frames, rows, heads = sizes
    chunks, _, _, _, width, wide = kv.shape
    per = wide // HD
    tokens = 2 * width
    f_at, r_at, h_at = (lax.axis_index(a) for a in ("frame", "row", "head"))
    frame_id = [(f_at - 1, r_at, h_at), (f_at + 1, r_at, h_at)]
    row_id = [(f_at, r_at - 1, h_at), (f_at, r_at + 1, h_at)]
    head_id = (f_at, r_at, 1 - h_at)
    has_f = [f_at > 0, f_at < frames - 1]
    has_r = [r_at > 0, r_at < rows - 1]

    loads = [
        pltpu.make_async_copy(src, dst, load_s.at[i])
        for i, (src, dst) in enumerate(
            (
                (q_hbm, q_ref), (k_hbm, k_ref), (v_hbm, v_ref), (kept_hbm, kept_ref),
                (gk_hbm, gk_ref.at[0]), (gq_hbm, gq_ref.at[0]), (t_hbm, t_ref),
            )
        )
    ]
    for load in loads:
        load.start()
    barrier = pltpu.get_barrier_semaphore()
    pl.semaphore_signal(barrier, inc=1, device_id=head_id, device_id_type=MESH)
    for s in (0, 1):
        for has, ids in ((has_f, frame_id), (has_r, row_id)):

            @pl.when(has[s])
            def _():
                pl.semaphore_signal(barrier, inc=1, device_id=ids[s], device_id_type=MESH)

    def remote(src, dst, send, recv, device):
        return pltpu.make_async_remote_copy(
            src_ref=src, dst_ref=dst, send_sem=send, recv_sem=recv,
            device_id=device, device_id_type=MESH,
        )

    def row_out(c, a, s):
        return remote(kv.at[c, a, 1, 1 + s], kv.at[c, a, 1, 3 - 3 * s],
                      row_s.at[c, a, s], row_r.at[c, a, 1 - s], row_id[s])

    def row_in(c, a, s):
        return remote(kv.at[c, a, 1, 1 + s], kv.at[c, a, 1, 3 * s],
                      row_s.at[c, a, s], row_r.at[c, a, s], row_id[s])

    def frame_out(c, a, s):
        return remote(kv.at[c, a, 1, pl.ds(1, 2)], kv.at[c, a, 2 - 2 * s, pl.ds(1, 2)],
                      fr_s.at[c, a, s], fr_r.at[c, a, 1 - s], frame_id[s])

    def frame_in(c, a, s):
        return remote(kv.at[c, a, 1, pl.ds(1, 2)], kv.at[c, a, 2 * s, pl.ds(1, 2)],
                      fr_s.at[c, a, s], fr_r.at[c, a, s], frame_id[s])

    def corner_out(c, a, s, t):
        return remote(kv.at[c, a, 1, 3 * t], kv.at[c, a, 2 - 2 * s, 3 * t],
                      co_s.at[c, a, s, t], co_r.at[c, a, 1 - s, t], frame_id[s])

    def corner_in(c, a, s, t):
        return remote(kv.at[c, a, 1, 3 * t], kv.at[c, a, 2 * s, 3 * t],
                      co_s.at[c, a, s, t], co_r.at[c, a, s, t], frame_id[s])

    def gx_copy(c, s, mine):
        return remote(gx_out.at[c, s], gx_in.at[c, s if mine else 1 - s],
                      gx_s.at[c, s], gx_r.at[c, s if mine else 1 - s], frame_id[s])

    def gy_copy(c, s, mine):
        return remote(gy_out.at[c, s], gy_in.at[c, s if mine else 1 - s],
                      gy_s.at[c, s], gy_r.at[c, s if mine else 1 - s], row_id[s])

    def w_copy():
        return remote(w_out, w_in, w_s.at[0], w_r.at[0], head_id)

    def wx_copy(s, mine):
        return remote(wx_out.at[s], wx_in.at[s if mine else 1 - s],
                      wx_s.at[s], wx_r.at[s if mine else 1 - s], frame_id[s])

    def wy_copy(s, mine):
        return remote(wy_out.at[s], wy_in.at[s if mine else 1 - s],
                      wy_s.at[s], wy_r.at[s if mine else 1 - s], row_id[s])

    def hx_copy(i):
        return remote(hx_out.at[i], hx_in.at[i], hx_s.at[i], hx_r.at[i], head_id)

    def lanes(c):
        return slice(c * wide, (c + 1) * wide)

    for s in (0, 1):

        @pl.when(jnp.logical_not(has_f[s]))
        def _():
            wx_in[s] = jnp.zeros((1, 4 * width), F32)

            def body(c, carry):
                kv[c, :, 2 * s] = jnp.zeros((2, 4, width, wide), BF16)
                gx_in[c, s] = jnp.zeros((2, 4, width, wide), BF16)
                return carry

            lax.fori_loop(0, chunks, body, 0)

        @pl.when(jnp.logical_not(has_r[s]))
        def _():
            wy_in[s] = jnp.zeros((1, 2 * width), F32)

            def body(c, carry):
                for a in (0, 1):
                    for d in range(3):
                        kv[c, a, d, 3 * s] = jnp.zeros((width, wide), BF16)
                gy_in[c, s] = jnp.zeros((2, width, wide), BF16)
                return carry

            lax.fori_loop(0, chunks, body, 0)

    loads[0].wait()
    loads[1].wait()
    square_q = jnp.zeros((tokens, 128), F32)
    square_k = jnp.zeros((tokens, 128), F32)
    for i in range(chunks * per):
        part = slice(i * HD, (i + 1) * HD)
        q_part = q_ref[0, :, :, part].reshape(tokens, HD).astype(F32)
        k_part = k_ref[0, :, :, part].reshape(tokens, HD).astype(F32)
        square_q += q_part * q_part
        square_k += k_part * k_part
    hx_out[0] = columns_to_rows(
        jnp.sum(square_q, -1, keepdims=True), jnp.sum(square_k, -1, keepdims=True)
    )

    loads[2].wait()
    for c in range(chunks):
        kv[c, 1, 1, 1:3] = v_ref[0, :, :, lanes(c)]
    peers = 1
    for edge in (*has_f, *has_r):
        peers = peers + edge.astype(jnp.int32)
    pl.semaphore_wait(barrier, peers)

    hx_copy(0).start()

    def send_own(c, a):
        for s in (0, 1):

            @pl.when(has_r[s])
            def _():
                row_out(c, a, s).start()

            @pl.when(has_f[s])
            def _():
                frame_out(c, a, s).start()

    def v_body(c, carry):
        send_own(c, 1)
        return carry

    lax.fori_loop(0, chunks, v_body, 0)

    def relay(a, c, carry):
        for t in (0, 1):

            @pl.when(has_r[t])
            def _():
                row_in(c, a, t).wait_recv()

            for s in (0, 1):

                @pl.when(jnp.logical_and(has_r[t], has_f[s]))
                def _():
                    corner_out(c, a, s, t).start()

        return carry

    loads[3].wait()
    keys = 12 * width
    key = lax.broadcasted_iota(jnp.int32, (1, keys), 1)
    key_line = key // TC
    kept_row = jnp.zeros((1, keys), jnp.int32)
    for d in range(3):
        frame = f_at + (d - 1)
        frame_ok = jnp.logical_and(frame >= 0, frame < frames)
        for g in range(4):
            row = 2 * r_at + (g - 1)
            ok = jnp.logical_and(frame_ok, jnp.logical_and(row >= 0, row < 2 * rows))
            for tile in range(TILES):
                one = kept_ref[jnp.clip(frame, 0, frames - 1), tile, jnp.clip(row, 0, 2 * rows - 1)]
                one = jnp.where(ok, one, 0)
                kept_row = jnp.where(key_line == (d * 4 + g) * TILES + tile, one, kept_row)
    query = lax.broadcasted_iota(jnp.int32, (tokens, keys), 0)
    keyb = lax.broadcasted_iota(jnp.int32, (tokens, keys), 1)
    q_row, q_tile = query // width + 1, (query % width) // TC
    k_line, k_tile = keyb // width, (keyb % width) // TC
    k_row = k_line % 4
    near = (jnp.abs(q_row - k_row) <= 1) & (jnp.abs(q_tile - k_tile) <= 1)
    same = (k_line == q_row + 4) & (q_tile == k_tile)
    kept_full = jnp.broadcast_to(kept_row, (tokens, keys)) > 0
    bias[...] = jnp.where(near & (kept_full | same), 0.0, NEG)

    lax.fori_loop(0, chunks, functools.partial(relay, 1), 0)
    for load in loads[4:]:
        load.wait()
    hx_copy(0).wait()
    scale_q, scale_k = rows_to_columns(
        lax.rsqrt((hx_out[0] + hx_in[0]) / features + norm_eps)
    )
    for c in range(chunks):
        k_norm = k_ref[0, :, :, lanes(c)].reshape(tokens, wide).astype(F32) * scale_k
        k_norm = (k_norm * gk_ref[:, lanes(c)]).astype(BF16)
        kv[c, 0, 1, 1:3] = k_norm.reshape(2, width, wide)
        send_own(c, 0)
    for c in range(chunks):
        q_norm = q_ref[0, :, :, lanes(c)].reshape(tokens, wide).astype(F32) * scale_q
        qn[c] = (q_norm * gq_ref[:, lanes(c)]).astype(BF16)

    lax.fori_loop(0, chunks, functools.partial(relay, 0), 0)

    acc[...] = jnp.zeros_like(acc)
    w_out[...] = jnp.zeros_like(w_out)

    def finish_x(c):
        for s in (0, 1):

            @pl.when(has_f[s])
            def _():
                gx_copy(c, s, True).wait_recv()

        for a in (0, 1):
            for g in range(4):
                total = own[c, a, g] + gx_in[c, 0, a, g].astype(F32) + gx_in[c, 1, a, g].astype(F32)
                if g in (0, 3):
                    gy_out[c, g // 3, a] = total.astype(BF16)
                else:
                    own[c, a, g] = total
        for s in (0, 1):

            @pl.when(has_r[s])
            def _():
                gy_copy(c, s, False).start()

    def compute(c, carry):
        for s in (0, 1):

            @pl.when(has_f[s])
            def _():
                for a in (0, 1):
                    frame_in(c, a, s).wait_recv()

            for t in (0, 1):

                @pl.when(jnp.logical_and(has_r[t], has_f[s]))
                def _():
                    for a in (0, 1):
                        corner_in(c, a, s, t).wait_recv()

        for j in range(per):
            part = slice(j * HD, (j + 1) * HD)
            at = pl.ds(pl.multiple_of(c * wide + j * HD, HD), HD)
            query_h = qn[c, :, part]
            key_h = kv[c, 0, :, :, :, part].reshape(keys, HD)
            value_h = kv[c, 1, :, :, :, part].reshape(keys, HD)
            inner = dot(query_h, key_h, COLS_T)
            scores = inner * (SCORE_SCALE * LOG2E) + bias[...]
            expo = jnp.exp2(scores - jnp.max(scores, -1, keepdims=True))
            prob = expo * (1.0 / jnp.sum(expo, -1, keepdims=True))
            prob_b = prob.astype(BF16)
            attended = dot(prob_b, value_h, PLAIN)
            target = t_ref[0, :, :, at].reshape(tokens, HD).astype(F32)
            d_out = (attended - target).astype(BF16)
            delta = jnp.sum(d_out.astype(F32) * attended, -1, keepdims=True)
            prob_grad = dot(d_out, value_h, COLS_T)
            score_grad = (prob * ((prob_grad - delta) * SCORE_SCALE)).astype(BF16)
            w_out[...] += jnp.sum(score_grad.astype(F32) * inner, 0, keepdims=True)
            dq_h = dot(score_grad, key_h, PLAIN)
            gated = dq_h * gq_ref[:, at]
            dq[c, :, part] = gated
            acc[...] += gated * q_ref[0, :, :, at].reshape(tokens, HD).astype(F32)
            for a, grad in (
                (0, dot(score_grad, query_h, ROWS_T)),
                (1, dot(prob_b, d_out, ROWS_T)),
            ):
                grad = grad.reshape(3, 4, width, HD)
                own[c, a, :, :, part] = grad[1]
                for s in (0, 1):
                    gx_out[c, s, a, :, :, part] = grad[2 * s].astype(BF16)
        for s in (0, 1):

            @pl.when(has_f[s])
            def _():
                gx_copy(c, s, False).start()

        @pl.when(c >= 2)
        def _():
            finish_x(c - 2)

        return carry

    lax.fori_loop(0, chunks, compute, 0)

    sum_q = jnp.sum(acc[...], -1, keepdims=True)
    hx_out[1] = columns_to_rows(sum_q, sum_q)
    w_copy().start()
    hx_copy(1).start()
    w_copy().wait()
    both = w_out[...] + w_in[...]
    for s in (0, 1):
        wx_out[s] = both[:, 8 * s * width : (8 * s + 4) * width]

        @pl.when(has_f[s])
        def _():
            wx_copy(s, False).start()

    hx_copy(1).wait()
    sum_q, _ = rows_to_columns((hx_out[1] + hx_in[1]) / features)
    back_q = scale_q * scale_q * scale_q * sum_q
    for c in range(chunks):
        q_float = q_ref[0, :, :, lanes(c)].reshape(tokens, wide).astype(F32)
        grad_q = scale_q * dq[c] - q_float * back_q
        oq_ref[0, :, :, lanes(c)] = grad_q.astype(BF16).reshape(2, width, wide)

    def last_x(c, carry):
        finish_x(c)
        return carry

    lax.fori_loop(max(chunks - 2, 0), chunks, last_x, 0)

    for s in (0, 1):

        @pl.when(has_f[s])
        def _():
            wx_copy(s, True).wait_recv()

    mine = both[:, 4 * width : 8 * width] + wx_in[0] + wx_in[1]
    halves = [mine[:, 0 : 2 * width], mine[:, 2 * width : 4 * width]]
    for s in (0, 1):
        wy_out[s] = halves[s]

        @pl.when(has_r[s])
        def _():
            wy_copy(s, False).start()

    def finish_y(c, carry):
        at = pl.ds(pl.multiple_of(c * wide, HD), wide)
        for s in (0, 1):

            @pl.when(has_r[s])
            def _():
                gy_copy(c, s, True).wait_recv()

        ov_ref[0, :, :, at] = (own[c, 1, 1:3] + gy_in[c, :, 1].astype(F32)).astype(BF16)
        gated = (own[c, 0, 1:3] + gy_in[c, :, 0].astype(F32)).reshape(tokens, wide) * gk_ref[:, at]
        own[c, 0, 1:3] = (gated * scale_k).reshape(2, width, wide)
        return carry

    lax.fori_loop(0, chunks, finish_y, 0)

    for s in (0, 1):

        @pl.when(has_r[s])
        def _():
            wy_copy(s, True).wait_recv()

    first, second = (
        jnp.broadcast_to(halves[s] + wy_in[s], (128, 128)).T for s in (0, 1)
    )
    sum_k = jnp.concatenate([first[width:], second[:width]], axis=0)[:, 0:1]
    back_k = scale_k * scale_k * sum_k / features
    for c in range(chunks):
        k_float = k_ref[0, :, :, lanes(c)].reshape(tokens, wide).astype(F32)
        grad_k = own[c, 0, 1:3].reshape(tokens, wide) - k_float * back_k
        ok_ref[0, :, :, lanes(c)] = grad_k.astype(BF16).reshape(2, width, wide)

    for s in (0, 1):

        @pl.when(has_f[s])
        def _():
            wx_copy(s, False).wait_send()

        @pl.when(has_r[s])
        def _():
            wy_copy(s, False).wait_send()

    def drain(c, carry):
        for s in (0, 1):

            @pl.when(has_r[s])
            def _():
                for a in (0, 1):
                    row_out(c, a, s).wait_send()
                gy_copy(c, s, False).wait_send()

            @pl.when(has_f[s])
            def _():
                for a in (0, 1):
                    frame_out(c, a, s).wait_send()
                gx_copy(c, s, False).wait_send()

            for t in (0, 1):

                @pl.when(jnp.logical_and(has_r[t], has_f[s]))
                def _():
                    for a in (0, 1):
                        corner_out(c, a, s, t).wait_send()

        return carry

    lax.fori_loop(0, chunks, drain, 0)


def hand_over(*refs):
    sources, results, (held, in_s, out_s) = refs[:3], refs[3:6], refs[6:]
    moves = [
        (
            pltpu.make_async_copy(sources[i], held.at[i], in_s.at[i]),
            pltpu.make_async_copy(held.at[i], results[i], out_s.at[i]),
        )
        for i in range(3)
    ]
    for take, _ in moves:
        take.start()
    for take, give in moves:
        take.wait()
        give.start()
    for _, give in moves:
        give.wait()


def per_device(sizes, per, q_pre, k_pre, values, target, gain_q, gain_k, kept):
    _, _, width, feat_dev = q_pre.shape
    chunks, wide = feat_dev // (per * HD), per * HD
    dma = pltpu.SemaphoreType.DMA
    vmem = pl.BlockSpec(memory_space=pltpu.VMEM)
    out = jax.ShapeDtypeStruct(q_pre.shape, BF16)
    grads = pl.pallas_call(
        functools.partial(kernel, sizes, feat_dev * sizes[2]),
        out_shape=(out, out, out),
        in_specs=[pl.BlockSpec(memory_space=pltpu.HBM)] * 7,
        out_specs=(vmem, vmem, vmem),
        scratch_shapes=[
            pltpu.VMEM((chunks, 2, 3, 4, width, wide), BF16),
            pltpu.VMEM((chunks, 2 * width, wide), BF16),
            pltpu.VMEM((2 * width, 12 * width), F32),
            pltpu.VMEM((chunks, 2, 2, 4, width, wide), BF16),
            pltpu.VMEM((chunks, 2, 2, 4, width, wide), BF16),
            pltpu.VMEM((chunks, 2, 2, width, wide), BF16),
            pltpu.VMEM((chunks, 2, 2, width, wide), BF16),
            pltpu.VMEM((chunks, 2, 4, width, wide), F32),
            pltpu.VMEM((chunks, 2 * width, wide), F32),
            pltpu.VMEM((2 * width, HD), F32),
            pltpu.VMEM((2, 8, 128), F32),
            pltpu.VMEM((2, 8, 128), F32),
            dma((chunks, 2, 2)),
            dma((chunks, 2, 2)),
            dma((chunks, 2, 2)),
            dma((chunks, 2, 2)),
            dma((chunks, 2, 2, 2)),
            dma((chunks, 2, 2, 2)),
            dma((chunks, 2)),
            dma((chunks, 2)),
            dma((chunks, 2)),
            dma((chunks, 2)),
            dma((2,)),
            dma((2,)),
            *([pltpu.VMEM(q_pre.shape, BF16)] * 4),
            pltpu.VMEM((1, feat_dev), F32),
            pltpu.VMEM((1, feat_dev), F32),
            pltpu.SMEM((kept.shape[0], TILES, kept.shape[1]), jnp.int32),
            dma((7,)),
            pltpu.VMEM((1, 12 * width), F32),
            pltpu.VMEM((1, 12 * width), F32),
            *([pltpu.VMEM((2, 1, 4 * width), F32)] * 2),
            *([pltpu.VMEM((2, 1, 2 * width), F32)] * 2),
            *([dma((1,))] * 2),
            *([dma((2,))] * 4),
        ],
        compiler_params=pltpu.CompilerParams(vmem_limit_bytes=60 << 20, collective_id=0, has_side_effects=True),
    )(q_pre, k_pre, values, target, gain_q, gain_k, kept.transpose(0, 2, 1))
    hbm = pl.BlockSpec(memory_space=pltpu.HBM)
    return pl.pallas_call(
        hand_over,
        out_shape=(out, out, out),
        in_specs=[hbm] * 3,
        out_specs=(hbm, hbm, hbm),
        scratch_shapes=[pltpu.VMEM((3, *q_pre.shape), BF16), dma((3,)), dma((3,))],
        compiler_params=pltpu.CompilerParams(vmem_limit_bytes=60 << 20),
    )(*grads)


def solution(mesh):
    sizes = tuple(mesh.shape[a] for a in ("frame", "row", "head"))
    grid = P("frame", "row", None, "head")
    return jax.shard_map(
        functools.partial(per_device, sizes, 2),
        mesh=mesh,
        in_specs=(grid, grid, grid, grid, P("head"), P("head"), P()),
        out_specs=(grid, grid, grid),
        check_vma=False,
    )
```
